256 devices in a mesh: dp: 32 (over z_lo, y, core), tensor: 8 (over x, z_hi).
Axes of the slice: x: 4, y: 4, z: 8 (z_hi: 2, z_lo: 4; z = z_hi * 4 + z_lo), core: 2. Of those that a mesh axis runs over, the one named last changes fastest.
Arguments:
- tokens: bfloat16 [8192, 8192], P(('dp', 'tensor')), may hold values from -6 to 6
- gain: float32 [8192], replicated, may hold values from 0.1 to 1.9
- stale: bfloat16 [8192, 2048], P(None, 'tensor'), may hold values from -0.0625 to 0.0625
- bias: float32 [2048], P('tensor'), may hold values from -3 to 3
- first: float32 [8192, 2048], P(('dp', 'tensor')), may hold values from -6 to 6
- second: float32 [8192, 2048], P(('dp', 'tensor')), may hold values from 0.1 to 10
- grad: float32 [8192, 2048], P(('dp', 'tensor')), may hold values from -6 to 6
- residual: float32 [8192, 2048], P(('dp', 'tensor')), may hold values from -0.12 to 0.12
- exponent: int32 [256, 16], P(('dp', 'tensor')), may hold values from 10 to 17
Outputs:
- new_first: float32 [8192, 2048], P(('dp', 'tensor'))
- new_second: float32 [8192, 2048], P(('dp', 'tensor'))
- projected: bfloat16 [8192, 2048], P('dp', 'tensor')
The draws below stay inside these ranges and needn't reach their ends.
All inputs are finite; a program needn't handle non-finite values.
Results may differ from the reference program's by a relative error of at most 0.0062.
Values may be sent and summed in bfloat16 or wider, within the bound.
A program may use at most 128 MiB of HBM per device.

```python
import math
import jax
import jax.numpy as jnp
from jax import lax

D = 8192
QROWS = 32
QCOL = 128
WIDE = 2048
TOKENS = 8192


def plant(drawn, own_key, smallest, largest):
    place = [jax.random.randint(jax.random.fold_in(own_key, axis), (), 0, length) for axis, length in enumerate(drawn.shape)]
    longest = drawn.shape.index(max(drawn.shape))
    next_to = place[:longest] + [(place[longest] + 1) % drawn.shape[longest]] + place[longest + 1:]
    return drawn.at[tuple(place)].set(smallest).at[tuple(next_to)].set(largest)


def level_of(stream_key, dims, split, smallest, largest):
    factor_of = 1.0
    for dim, parts in split:
        draws = jax.random.uniform(jax.random.fold_in(jax.random.fold_in(stream_key, 6), dim), (parts,), jnp.float32, smallest / len(split), largest / len(split))
        factor_of = factor_of * jnp.repeat(jnp.exp(draws), dims[dim] // parts).reshape((-1,) + (1,) * (len(dims) - 1 - dim))
    return factor_of


def gaussian(rng, extent, scale, most, split=(), kind=jnp.bfloat16):
    entries = jax.random.normal(rng, extent, jnp.float32) * scale
    if len(split) > 0:
        entries = level_of(rng, extent, split, -0.22, 0.18) * entries
    return jnp.clip(entries, min=-most, max=most).astype(kind)


def setup_inputs(seed: int = 0) -> dict:
    key_list = jax.random.split(jax.random.key(seed), 10)
    return {
        "tokens": gaussian(key_list[0], (TOKENS, D), 1.0, 6.0, ((0, 256),)),
        "gain": jnp.clip(1.0 + 0.18 * jax.random.normal(key_list[1], (D,), jnp.float32), 0.1, 1.9),
        "stale": gaussian(key_list[2], (D, WIDE), D ** -0.5, 0.0625, ((1, 8),)),
        "bias": gaussian(key_list[3], (WIDE,), 0.5, 3.0, ((0, 8),), jnp.float32),
        "first": gaussian(key_list[4], (D, WIDE), 1.0, 6.0, ((0, 256),), jnp.float32),
        "second": jnp.clip(jnp.exp(math.log(10.0) - 4.6051702 * jax.random.uniform(key_list[5], (D, WIDE), jnp.float32) ** level_of(key_list[5], (D, WIDE), ((0, 256),), -0.2, 0.2)), 0.1, 10.0),
        "grad": gaussian(key_list[6], (D, WIDE), 1.0, 6.0, ((0, 256),), jnp.float32),
        "residual": gaussian(key_list[7], (D, WIDE), 0.02, 0.12, ((0, 256),), jnp.float32),
        "exponent": plant(jax.random.randint(key_list[8], (D // QROWS, WIDE // QCOL), 10, 18), jax.random.fold_in(key_list[8], 1), 10, 17).astype(jnp.int32),
    }


def reference(tokens, gain, stale, bias, first, second, grad, residual, exponent):
    new_first = 0.9 * first + 0.1 * grad
    new_second = 0.95 * second + 0.05 * grad * grad
    corrected = 0.02 * new_first / (jnp.sqrt(new_second) + 1e-08) + residual
    expo = exponent.astype(jnp.float32)
    upward = jnp.exp2(expo)[:, None, :, None]
    downward = jnp.exp2(-expo)[:, None, :, None]
    blocks_rows = exponent.shape[0]
    blocks_cols = exponent.shape[1]
    blocked = corrected.reshape(blocks_rows, QROWS, blocks_cols, QCOL) * upward
    quant = jnp.clip(blocked, -448.0, 448.0).astype(jnp.bfloat16)
    quant = lax.optimization_barrier(quant)
    delta = (quant.astype(jnp.float32) * downward).reshape(D, WIDE).astype(jnp.bfloat16)
    weight = (stale.astype(jnp.float32) + delta.astype(jnp.float32)).astype(jnp.bfloat16)
    values = tokens.astype(jnp.float32)
    meansq = lax.optimization_barrier(jnp.mean(values * values, axis=1, keepdims=True))
    normed = (values * lax.rsqrt(meansq + 1e-06) * gain[None, :]).astype(jnp.bfloat16)
    product = jnp.dot(normed, weight, preferred_element_type=jnp.float32)
    projected = (product + bias[None, :]).astype(jnp.bfloat16)
    return (new_first, new_second, projected)
```

```python
import functools

import jax
import jax.numpy as jnp
from jax import lax
from jax.experimental import pallas as pl
from jax.experimental.pallas import tpu as pltpu
from jax.sharding import PartitionSpec as P

MESH = pl.DeviceIdType.MESH
X, Y, ZL, ZH, C = 4, 4, 4, 2, 2
Z = ZL * ZH
RB = 32
KS = 2048
NB = 512
HC = 256


def ids():
    table, count = {}, 0

    def add(*key):
        nonlocal count
        table[key] = count
        count += 1

    for i in range(1, 8):
        add("stale", i)
    for i in range(1, 4):
        add("y", i)
        add("r", i)
        add("wx", i)
    for p in range(4):
        add("xr", p)
        add("xl", p)
    for p in (0, 3):
        add("fr", p)
    for p in (1, 2):
        add("fl", p)
    for d in range(4):
        for h in range(2):
            add("zr", d, h)
            add("zl", d, h)
    for d in range(5):
        for h in range(2):
            add("sr", d, h)
            add("sl", d, h)
    for b in range(4):
        add("zx", b)
        for dy in range(1, 4):
            add("c", b, dy)
    return table, count


IDS, NIDS = ids()


def kernel(
    tok_ref, gain_ref, stale_ref, first_ref, second_ref, grad_ref, resid_ref, expo_ref,
    out_ref,
    tok, wbuf, sin, delta, wsend, rbuf, rsend, cf, cb, cin, zs, zin, send, recv, loc,
):
    dp = lax.axis_index("dp")
    t = lax.axis_index("tensor")
    c = lax.rem(dp, C)
    y = lax.rem(dp // C, Y)
    zl = dp // (C * Y)
    x = t // ZH
    zh = lax.rem(t, ZH)
    z = zh * ZL + zl

    def at(x_=None, y_=None, z_=None, c_=None):
        x_ = x if x_ is None else x_
        y_ = y if y_ is None else y_
        z_ = z if z_ is None else z_
        c_ = c if c_ is None else c_
        return ((lax.rem(z_, ZL) * Y + y_) * C + c_, x_ * ZH + z_ // ZL)

    xs = [lax.rem(x + i, X) for i in range(X)]
    ys = [lax.rem(y + i, Y) for i in range(Y)]
    zs_ = [lax.rem(z + i, Z) for i in range(Z)]
    ts = [lax.rem(t + i, 8) for i in range(8)]

    def copy(src, dst, dev, *key):
        i = IDS[key]
        return pltpu.make_async_remote_copy(
            src_ref=src, dst_ref=dst, send_sem=send.at[i], recv_sem=recv.at[i],
            device_id=dev, device_id_type=MESH,
        )

    sent = []

    def start(src, dst, dev, *key):
        copy(src, dst, dev, *key).start()
        sent.append((src, dst, dev, key))

    def arrived(ref, *key):
        copy(ref, ref, (dp, t), *key).wait_recv()

    barrier = pltpu.get_barrier_semaphore()
    partners = (
        [(dp, ts[i]) for i in range(1, 8)]
        + [at(y_=ys[i]) for i in range(1, 4)]
        + [at(z_=zs_[1]), at(z_=zs_[7]), at(c_=1 - c)]
    )
    for dev in partners:
        pl.semaphore_signal(barrier, inc=1, device_id=dev, device_id_type=MESH)
    pl.semaphore_wait(barrier, len(partners))

    for i in range(1, 8):
        rows = pl.ds(pl.multiple_of(dp * 256 + ts[i] * RB, RB), RB)
        start(stale_ref.at[rows, :], sin.at[t], (dp, ts[i]), "stale", i)
    rows = pl.ds(pl.multiple_of(dp * 256 + t * RB, RB), RB)
    own_stale = pltpu.make_async_copy(stale_ref.at[rows, :], sin.at[t], loc.at[0])
    own_stale.start()

    def part(k, y_):
        return tok_ref.at[:, pl.ds(pl.multiple_of(k * 2048 + y_ * 512, 512), 512)]

    def spread(dev, y_, *key):
        i = IDS[key]
        for k in range(ZL):
            pltpu.make_async_remote_copy(
                src_ref=part(k, y_), dst_ref=tok.at[x, y, :, pl.ds(k * 512, 512)],
                send_sem=send.at[i], recv_sem=recv.at[i], device_id=dev, device_id_type=MESH,
            ).start()
        sent.append((tok.at[x, y], tok.at[x, y], dev, key))

    spread(at(x_=xs[1]), y, "xr", 0)
    spread(at(x_=xs[3]), y, "xl", 0)
    for dy in (1, 3, 2):
        spread(at(y_=ys[dy]), ys[dy], "y", dy)
    for k in range(ZL):
        pltpu.make_async_copy(part(k, y), tok.at[x, y, :, pl.ds(k * 512, 512)], loc.at[1]).start()

    total = jnp.zeros((RB, 1), jnp.float32)
    for k in range(8):
        v = tok_ref[:, k * 1024:(k + 1) * 1024].astype(jnp.float32)
        total = total + jnp.sum(v * v, axis=1, keepdims=True)
    scale = lax.rsqrt(total / 8192.0 + 1e-06)
    rsend[...] = jnp.broadcast_to(scale, (RB, 128))
    for dx in range(1, 4):
        start(rsend, rbuf.at[dx], at(x_=xs[dx]), "r", dx)

    for j in range(16):
        cols = slice(j * 128, (j + 1) * 128)
        g = grad_ref[:, cols]
        nf = 0.9 * first_ref[:, cols] + 0.1 * g
        ns = 0.95 * second_ref[:, cols] + 0.05 * g * g
        corrected = 0.02 * nf / (jnp.sqrt(ns) + 1e-08) + resid_ref[:, cols]
        e = jnp.broadcast_to(expo_ref[:, j:j + 1], (RB, 128))
        up = lax.shift_left(jnp.ones_like(e), e).astype(jnp.float32)
        down = lax.shift_left(jnp.ones_like(e), 30 - e).astype(jnp.float32) * (2.0 ** -30)
        q = jnp.clip(corrected * up, -448.0, 448.0).astype(jnp.bfloat16)
        delta[:, cols] = q.astype(jnp.float32) * down

    block = dp * 8 + t
    grow = jnp.broadcast_to(gain_ref[pl.ds(block // 4, 1), :], (RB, 128))
    lane = lax.broadcasted_iota(jnp.int32, (RB, 128), 1)
    row = lax.broadcasted_iota(jnp.int32, (RB, 128), 0)
    hit = lane == row + lax.rem(block, 4) * RB
    gcol = jnp.sum(jnp.where(hit, grow, 0.0), axis=1, keepdims=True)

    own_stale.wait()
    for i in range(1, 8):
        arrived(sin.at[lax.rem(t + 8 - i, 8)], "stale", i)
    for tt in range(8):
        w = gcol * (sin[tt].astype(jnp.float32) + delta[:, tt * HC:(tt + 1) * HC])
        wsend[tt // 2, :, (tt % 2) * HC:(tt % 2 + 1) * HC] = w.astype(jnp.bfloat16)
    for dx in range(1, 4):
        start(wsend.at[xs[dx]], wbuf.at[zl, c, x, zh], at(x_=xs[dx]), "wx", dx)
    own_w = pltpu.make_async_copy(wsend.at[x], wbuf.at[zl, c, x, zh], loc.at[2])
    own_w.start()
    own_w.wait()

    right, left = at(x_=xs[1]), at(x_=xs[3])

    def from_y(p):
        ref = tok.at[x, ys[(4 - p) % 4]]
        arrived(ref, "y", p)
        start(ref, ref, right, "xr", p)
        start(ref, ref, left, "xl", p)

    def from_left(p):
        ref = tok.at[xs[3], ys[(4 - p) % 4]]
        arrived(ref, "xr", p)
        if p in (0, 3):
            start(ref, ref, right, "fr", p)

    def from_right(p):
        ref = tok.at[xs[1], ys[(4 - p) % 4]]
        arrived(ref, "xl", p)
        if p in (1, 2):
            start(ref, ref, left, "fl", p)

    up_z, down_z, sibling = at(z_=zs_[1]), at(z_=zs_[7]), at(c_=1 - c)

    def blk(i, core, h):
        z_ = zs_[i % Z]
        return wbuf.at[lax.rem(z_, ZL), core, pl.ds(2 * h, 2), z_ // ZL]

    def own_block():
        for dx in range(1, 4):
            arrived(wbuf.at[zl, c, xs[4 - dx], zh], "wx", dx)
        for h in range(2):
            ref = blk(0, c, h)
            start(ref, ref, up_z, "zr", 0, h)
            start(ref, ref, down_z, "zl", 0, h)
        for h in range(2):
            ref = blk(0, c, h)
            start(ref, ref, sibling, "sr", 0, h)

    def ring(d):
        for h in range(2):
            if d < 4 or h == 0:
                ref = blk(Z - d, c, h)
                arrived(ref, "zr", d - 1, h)
                if d < 3 or (d == 3 and h == 0):
                    start(ref, ref, up_z, "zr", d, h)
                start(ref, ref, sibling, "sr", d, h)
            if d < 4 or h == 1:
                ref = blk(d, c, h)
                arrived(ref, "zl", d - 1, h)
                if d < 3 or (d == 3 and h == 1):
                    start(ref, ref, down_z, "zl", d, h)
                start(ref, ref, sibling, "sl", d, h)

    from_y(1)
    from_y(3)
    own_block()
    from_left(0)
    from_y(2)
    from_right(1)
    ring(1)
    from_left(3)
    ring(2)
    from_right(2)
    ring(3)
    ring(4)
    for d in range(5):
        for h in range(2):
            if d < 4 or h == 0:
                arrived(blk(Z - d, 1 - c, h), "sr", d, h)
            if 0 < d < 4 or (d == 4 and h == 1):
                arrived(blk(d, 1 - c, h), "sl", d, h)

    def product(b, x_):
        a = tok[x_].reshape(Y * RB, KS)
        w = wbuf[...].reshape(KS, NB)
        acc = jnp.dot(a, w, preferred_element_type=jnp.float32)
        cf[b] = acc.reshape(Y, RB, NB)
        cb[b] = acc.astype(jnp.bfloat16).reshape(Y, RB, NB)
        for dy in (1, 3, 2):
            start(cb.at[b, ys[dy]], cin.at[b, dy], at(y_=ys[dy]), "c", b, dy)

    partner = at(z_=zs_[4])

    def finish(b, x_):
        v = cf[b, y]
        for dy in (1, 3, 2):
            arrived(cin.at[b, dy], "c", b, dy)
            v = v + cin[b, dy].astype(jnp.float32)
        if b == 0:
            r = rsend[...]
        else:
            dx = (1, 3, 2)[b - 1]
            arrived(rbuf.at[dx], "r", dx)
            r = rbuf[dx]
        v = v * r[:, :1]
        cf[b, 0, :, :HC] = v[:, :HC]
        cf[b, 1, :, :HC] = v[:, HC:]
        zs[b, 0] = v[:, :HC].astype(jnp.bfloat16)
        zs[b, 1] = v[:, HC:].astype(jnp.bfloat16)
        start(zs.at[b, 1 - zh], zin.at[b], partner, "zx", b)
        out_ref[x_ * 2 + zh] = cf[b, zh, :, :HC]

    pltpu.make_async_copy(tok.at[x, y], tok.at[x, y], loc.at[1]).wait()
    order = (x, xs[3], xs[1], xs[2])
    product(0, order[0])
    for p in (1, 2):
        from_left(p)
    product(1, order[1])
    for p in (0, 3):
        from_right(p)
    product(2, order[2])
    finish(0, order[0])
    finish(1, order[1])
    for p in (0, 3):
        arrived(tok.at[xs[2], ys[(4 - p) % 4]], "fr", p)
    for p in (1, 2):
        arrived(tok.at[xs[2], ys[(4 - p) % 4]], "fl", p)
    product(3, order[3])
    finish(2, order[2])
    finish(3, order[3])
    for b in range(4):
        arrived(zin.at[b], "zx", b)
        out_ref[order[b] * 2 + 1 - zh] = zin[b].astype(jnp.float32)
    for src, dst, dev, key in sent:
        copy(src, dst, dev, *key).wait_send()


def on_device(tokens, gain, stale, bias, first, second, grad, residual, exponent):
    new_first = 0.9 * first + 0.1 * grad
    new_second = 0.95 * second + 0.05 * grad * grad
    vmem = pl.BlockSpec(memory_space=pltpu.VMEM)
    out = pl.pallas_call(
        kernel,
        out_shape=jax.ShapeDtypeStruct((8, RB, HC), jnp.float32),
        in_specs=[vmem, vmem, pl.BlockSpec(memory_space=pl.ANY)] + [vmem] * 5,
        out_specs=vmem,
        scratch_shapes=[
            pltpu.VMEM((X, Y, RB, KS), jnp.bfloat16),
            pltpu.VMEM((ZL, C, X, ZH, RB, NB), jnp.bfloat16),
            pltpu.VMEM((8, RB, HC), jnp.bfloat16),
            pltpu.VMEM((RB, 2048), jnp.float32),
            pltpu.VMEM((X, RB, NB), jnp.bfloat16),
            pltpu.VMEM((X, RB, 128), jnp.float32),
            pltpu.VMEM((RB, 128), jnp.float32),
            pltpu.VMEM((4, Y, RB, NB), jnp.float32),
            pltpu.VMEM((4, Y, RB, NB), jnp.bfloat16),
            pltpu.VMEM((4, Y, RB, NB), jnp.bfloat16),
            pltpu.VMEM((4, 2, RB, HC), jnp.bfloat16),
            pltpu.VMEM((4, RB, HC), jnp.bfloat16),
            pltpu.SemaphoreType.DMA((NIDS,)),
            pltpu.SemaphoreType.DMA((NIDS,)),
            pltpu.SemaphoreType.DMA((3,)),
        ],
        compiler_params=pltpu.CompilerParams(collective_id=0, has_side_effects=True),
    )(tokens, gain.reshape(64, 128), stale, first, second, grad, residual, exponent)
    projected = (out.reshape(256, HC) + bias[None, :]).astype(jnp.bfloat16)
    return (new_first, new_second, projected)


def solution(mesh):
    return jax.shard_map(
        on_device,
        mesh=mesh,
        in_specs=(
            P(("dp", "tensor"), None),
            P(),
            P(None, "tensor"),
            P("tensor"),
            P(("dp", "tensor"), None),
            P(("dp", "tensor"), None),
            P(("dp", "tensor"), None),
            P(("dp", "tensor"), None),
            P(("dp", "tensor"), None),
        ),
        out_specs=(P(("dp", "tensor"), None), P(("dp", "tensor"), None), P("dp", "tensor")),
        check_vma=False,
    )
```

```python
import jax
import jax.numpy as jnp
from jax import lax
from jax.experimental import pallas as pl
from jax.experimental.pallas import tpu as pltpu
from jax.sharding import PartitionSpec as P

MESH = pl.DeviceIdType.MESH
X, Y, ZL, ZH, C = 4, 4, 4, 2, 2
Z = ZL * ZH
RB = 32
KS = 2048
HC = 256


def ids():
    table = {}

    def add(*key):
        table[key] = len(table)

    add("stale")
    for i in range(1, 4):
        add("y", i)
        add("r", i)
        add("d", i)
    for p in range(4):
        add("xr", p)
        add("xl", p)
    add("fr", 1)
    add("fl", 3)
    for p in (0, 2):
        add("fr", p)
        add("fl", p)
    for d in range(4):
        for g in range(4):
            if d < 3 or g < 2:
                add("zr", d, g)
            if d < 3 or g >= 2:
                add("zl", d, g)
    for d in range(5):
        add("sr", d)
        if d:
            add("sl", d)
    for b in range(4):
        add("zx", b)
        for dy in range(1, 4):
            add("c", b, dy)
    return table


IDS = ids()


def kernel(
    tok_in, gain_ref, stale_ref, bias_ref, first_in, second_in, grad_in, resid_in, expo_ref,
    out_ref,
    tokv, first_ref, second_ref, grad_ref, resid_ref,
    tok, wbuf, sloc, spart, dsend, drecv, rbuf, rsend, cf, cb, cin, zs, zin, send, recv, loc,
):
    dp = lax.axis_index("dp")
    t = lax.axis_index("tensor")
    c = lax.rem(dp, C)
    y = lax.rem(dp // C, Y)
    zl = dp // (C * Y)
    x = t // ZH
    zh = lax.rem(t, ZH)
    z = zh * ZL + zl

    def at(x_=None, y_=None, z_=None, c_=None):
        x_ = x if x_ is None else x_
        y_ = y if y_ is None else y_
        z_ = z if z_ is None else z_
        c_ = c if c_ is None else c_
        return ((lax.rem(z_, ZL) * Y + y_) * C + c_, x_ * ZH + z_ // ZL)

    xs = [lax.rem(x + i, X) for i in range(X)]
    ys = [lax.rem(y + i, Y) for i in range(Y)]
    zr = [lax.rem(z + i, Z) for i in range(Z)]
    right, left = at(x_=xs[1]), at(x_=xs[3])
    up_z, down_z, sibling = at(z_=zr[1]), at(z_=zr[7]), at(c_=1 - c)
    mirror, partner = at(z_=Z - 1 - z), at(z_=zr[4])

    def copy(src, dst, dev, *key):
        i = IDS[key]
        return pltpu.make_async_remote_copy(
            src_ref=src, dst_ref=dst, send_sem=send.at[i], recv_sem=recv.at[i],
            device_id=dev, device_id_type=MESH,
        )

    sent = []

    def start(src, dst, dev, *key):
        copy(src, dst, dev, *key).start()
        sent.append((dst, dev, key))

    def arrived(ref, *key):
        copy(ref, ref, right, *key).wait_recv()

    barrier = pltpu.get_barrier_semaphore()
    partners = (
        [mirror, at(x_=xs[2]), at(y_=ys[2]), up_z, down_z, right, left]
        + [at(y_=ys[1]), at(y_=ys[3]), sibling]
    )
    for dev in partners:
        pl.semaphore_signal(barrier, inc=1, device_id=dev, device_id_type=MESH)

    loads = []
    for i, (src, dst) in enumerate((
        (first_in, first_ref), (second_in, second_ref), (grad_in, grad_ref),
        (resid_in, resid_ref), (tok_in, tokv),
    )):
        loads.append(pltpu.make_async_copy(src, dst, loc.at[i]))
        loads[-1].start()

    def stale_rows(dp_, xp, zh_):
        return stale_ref.at[pl.ds(pl.multiple_of(dp_ * 256 + xp * 64 + zh_ * RB, RB), RB), :]

    for xp in range(X):
        pltpu.make_async_copy(stale_rows(dp, xp, zh), sloc.at[xp], loc.at[5]).start()

    for load in loads[:4]:
        load.wait()
    for j in range(16):
        cols = slice(j * 128, (j + 1) * 128)
        g = grad_ref[:, cols]
        nf = 0.9 * first_ref[:, cols] + 0.1 * g
        ns = 0.95 * second_ref[:, cols] + 0.05 * g * g
        corrected = 0.02 * nf / (jnp.sqrt(ns) + 1e-08) + resid_ref[:, cols]
        e = jnp.broadcast_to(expo_ref[:, j:j + 1], (RB, 128))
        up = lax.shift_left(jnp.ones_like(e), e).astype(jnp.float32)
        down = lax.shift_left(jnp.ones_like(e), 30 - e).astype(jnp.float32) * (2.0 ** -30)
        q = jnp.clip(corrected * up, -448.0, 448.0).astype(jnp.bfloat16)
        dsend[j // 4, (j // 2) % 2, :, (j % 2) * 128:(j % 2 + 1) * 128] = (
            q.astype(jnp.float32) * down
        ).astype(jnp.bfloat16)

    lane = lax.broadcasted_iota(jnp.int32, (RB, 128), 1)
    row = lax.broadcasted_iota(jnp.int32, (RB, 128), 0)
    gcol = []
    for xp in range(X):
        grow = jnp.broadcast_to(gain_ref[pl.ds(dp * 2 + xp // 2, 1), :], (RB, 128))
        hit = lane == row + (xp % 2) * 64 + zh * RB
        gcol.append(jnp.sum(jnp.where(hit, grow, 0.0), axis=1, keepdims=True))

    loads[4].wait()
    total = jnp.zeros((RB, 1), jnp.float32)
    for k in range(8):
        v = tokv[:, k * 1024:(k + 1) * 1024].astype(jnp.float32)
        total = total + jnp.sum(v * v, axis=1, keepdims=True)
    rsend[...] = jnp.broadcast_to(lax.rsqrt(total / 8192.0 + 1e-06), (RB, 128))

    pl.semaphore_wait(barrier, len(partners))

    for dx in (1, 3, 2):
        start(dsend.at[xs[dx]], drecv.at[dx], at(x_=xs[dx]), "d", dx)
    dp_m = ((ZL - 1 - zl) * Y + y) * C + c
    for xp in range(X):
        copy(stale_rows(dp_m, xp, 1 - zh), spart.at[xp], mirror, "stale").start()
    sent.append((spart, mirror, ("stale",)))

    def part(k, y_):
        return tokv.at[:, pl.ds(pl.multiple_of(k * 2048 + y_ * 512, 512), 512)]

    def spread(dev, y_, *key):
        for k in range(ZL):
            copy(part(k, y_), tok.at[x, y, :, pl.ds(k * 512, 512)], dev, *key).start()
        sent.append((tok.at[x, y], dev, key))

    spread(at(y_=ys[1]), ys[1], "y", 1)
    spread(at(y_=ys[3]), ys[3], "y", 3)
    spread(right, y, "xr", 0)
    spread(left, y, "xl", 0)
    spread(at(y_=ys[2]), ys[2], "y", 2)
    for k in range(ZL):
        pltpu.make_async_copy(part(k, y), tok.at[x, y, :, pl.ds(k * 512, 512)], loc.at[6]).start()
    for dx in range(1, 4):
        start(rsend, rbuf.at[dx], at(x_=xs[dx]), "r", dx)

    def merge(dx, half, stale):
        xp = xs[(4 - dx) % 4]
        d = dsend[xp, half] if dx == 0 else drecv[dx, half]
        g = gcol[3]
        for i in range(3):
            g = jnp.where(xp == i, gcol[i], g)
        w = g * (stale[xp].astype(jnp.float32) + d.astype(jnp.float32))
        wbuf[zl, c, xp, zh, half] = w.astype(jnp.bfloat16)

    def piece(i, g):
        z_ = zr[i % Z]
        zh_ = z_ // ZL
        half = zh_ if g < 2 else 1 - zh_
        return wbuf.at[lax.rem(z_, ZL), c, pl.ds(2 * (g % 2), 2), zh_, half]

    def whole(i, core):
        z_ = zr[i % Z]
        return wbuf.at[lax.rem(z_, ZL), core, :, z_ // ZL]

    def half_of(i, core, other):
        z_ = zr[i % Z]
        zh_ = z_ // ZL
        return wbuf.at[lax.rem(z_, ZL), core, :, zh_, 1 - zh_ if other else zh_]

    pltpu.make_async_copy(sloc, sloc, loc.at[5]).wait()
    merge(0, zh, sloc)
    for dx in (1, 3, 2):
        arrived(drecv.at[dx], "d", dx)
        merge(dx, zh, sloc)
    for g in range(2):
        start(piece(0, g), piece(0, g), up_z, "zr", 0, g)
        start(piece(0, g), piece(0, g), down_z, "zl", 0, g)
    arrived(spart, "stale")
    for dx in range(4):
        merge(dx, 1 - zh, spart)
    for g in range(2, 4):
        start(piece(0, g), piece(0, g), up_z, "zr", 0, g)
        start(piece(0, g), piece(0, g), down_z, "zl", 0, g)
    start(whole(0, c), whole(0, c), sibling, "sr", 0)

    def from_y(p):
        ref = tok.at[x, ys[(4 - p) % 4]]
        arrived(ref, "y", p)
        start(ref, ref, right, "xr", p)
        start(ref, ref, left, "xl", p)

    def token(i, p, rows=None):
        ref = tok.at[xs[i], ys[(4 - p) % 4]]
        return ref if rows is None else ref.at[pl.ds(rows, RB // 2), :]

    def ring(d):
        for g in range(4):
            if d < 4 or g < 2:
                ref = piece(Z - d, g)
                arrived(ref, "zr", d - 1, g)
                if d < 3 or (d == 3 and g < 2):
                    start(ref, ref, up_z, "zr", d, g)
            if d < 4 or g >= 2:
                ref = piece(d, g)
                arrived(ref, "zl", d - 1, g)
                if d < 3 or (d == 3 and g >= 2):
                    start(ref, ref, down_z, "zl", d, g)
        if d < 4:
            start(whole(Z - d, c), whole(Z - d, c), sibling, "sr", d)
            start(whole(d, c), whole(d, c), sibling, "sl", d)
        else:
            start(half_of(4, c, 0), half_of(4, c, 0), sibling, "sr", d)
            start(half_of(4, c, 1), half_of(4, c, 1), sibling, "sl", d)

    from_y(1)
    from_y(3)
    ring(1)
    from_y(2)
    ring(2)
    arrived(token(3, 1), "xr", 1)
    start(token(3, 1), token(3, 1), right, "fr", 1)
    arrived(token(1, 3), "xl", 3)
    start(token(1, 3), token(1, 3), left, "fl", 3)
    ring(3)
    for p in (2, 0):
        arrived(token(3, p), "xr", p)
        start(token(3, p, 0), token(3, p, 0), right, "fr", p)
        arrived(token(1, p), "xl", p)
        start(token(1, p, 16), token(1, p, 16), left, "fl", p)
    ring(4)
    for d in range(4):
        arrived(whole(Z - d, 1 - c), "sr", d)
        if d:
            arrived(whole(d, 1 - c), "sl", d)
    arrived(half_of(4, 1 - c, 0), "sr", 4)
    arrived(half_of(4, 1 - c, 1), "sl", 4)

    def weights(half):
        return wbuf[:, :, :, :, half].reshape(KS, HC)

    def send_partial(b, dy):
        start(cb.at[b, ys[dy]], cin.at[b, dy], at(y_=ys[dy]), "c", b, dy)

    def product(b, x_):
        a = tok[x_].reshape(Y * RB, KS)
        for half in range(2):
            acc = jnp.dot(a, weights(half), preferred_element_type=jnp.float32)
            acc = acc.reshape(Y, RB, HC)
            cf[b, :, half] = acc
            cb[b, :, half] = acc.astype(jnp.bfloat16)
        for dy in (1, 3, 2):
            send_partial(b, dy)

    order = (x, xs[3], xs[1], xs[2])

    def finish(b):
        if b == 0:
            r = rsend[:, :1]
        else:
            dx = (1, 3, 2)[b - 1]
            arrived(rbuf.at[dx], "r", dx)
            r = rbuf[dx, :, :1]
        for dy in (1, 3, 2):
            arrived(cin.at[b, dy], "c", b, dy)

        def total_of(half):
            v = cf[b, y, half]
            for dy in range(1, 4):
                v = v + cin[b, dy, half].astype(jnp.float32)
            return v * r

        zs[b] = total_of(1 - zh).astype(jnp.bfloat16)
        start(zs.at[b], zin.at[b], partner, "zx", b)
        out_ref[order[b] * 2 + zh] = (total_of(zh) + bias_ref[...]).astype(jnp.bfloat16)

    pltpu.make_async_copy(tok.at[x, y], tok.at[x, y], loc.at[6]).wait()
    product(0, order[0])
    arrived(token(3, 3), "xr", 3)
    product(1, order[1])
    arrived(token(1, 1), "xl", 1)
    product(2, order[2])
    arrived(token(2, 1), "fr", 1)
    arrived(token(2, 3), "fl", 3)
    arrived(token(2, 2, 0), "fr", 2)
    arrived(token(2, 2, 16), "fl", 2)
    a = jnp.concatenate([tok[xs[2], ys[dy]] for dy in (1, 2, 3)], axis=0)
    for half in range(2):
        acc = jnp.dot(a, weights(half), preferred_element_type=jnp.float32)
        for i, dy in enumerate((1, 2, 3)):
            cb[3, ys[dy], half] = acc[i * RB:(i + 1) * RB].astype(jnp.bfloat16)
    for dy in (1, 3, 2):
        send_partial(3, dy)
    for b in range(3):
        finish(b)
    arrived(token(2, 0, 0), "fr", 0)
    arrived(token(2, 0, 16), "fl", 0)
    a = tok[xs[2], y]
    for half in range(2):
        cf[3, y, half] = jnp.dot(a, weights(half), preferred_element_type=jnp.float32)
    finish(3)
    for b in range(4):
        arrived(zin.at[b], "zx", b)
        out_ref[order[b] * 2 + 1 - zh] = (
            zin[b].astype(jnp.float32) + bias_ref[...]
        ).astype(jnp.bfloat16)
    for dst, dev, key in sent:
        copy(dst, dst, dev, *key).wait_send()


def on_device(tokens, gain, stale, bias, first, second, grad, residual, exponent):
    new_first = 0.9 * first + 0.1 * grad
    new_second = 0.95 * second + 0.05 * grad * grad
    vmem = pl.BlockSpec(memory_space=pltpu.VMEM)
    there = pl.BlockSpec(memory_space=pl.ANY)
    bf16, f32 = jnp.bfloat16, jnp.float32
    out = pl.pallas_call(
        kernel,
        out_shape=jax.ShapeDtypeStruct((8, RB, HC), bf16),
        in_specs=[there, vmem, there, vmem, there, there, there, there, vmem],
        out_specs=vmem,
        scratch_shapes=[
            pltpu.VMEM((RB, 8192), bf16),
            pltpu.VMEM((RB, 2048), f32),
            pltpu.VMEM((RB, 2048), f32),
            pltpu.VMEM((RB, 2048), f32),
            pltpu.VMEM((RB, 2048), f32),
            pltpu.VMEM((X, Y, RB, KS), bf16),
            pltpu.VMEM((ZL, C, X, ZH, 2, RB, HC), bf16),
            pltpu.VMEM((X, RB, HC), bf16),
            pltpu.VMEM((X, RB, HC), bf16),
            pltpu.VMEM((X, 2, RB, HC), bf16),
            pltpu.VMEM((X, 2, RB, HC), bf16),
            pltpu.VMEM((X, RB, 128), f32),
            pltpu.VMEM((RB, 128), f32),
            pltpu.VMEM((4, Y, 2, RB, HC), f32),
            pltpu.VMEM((4, Y, 2, RB, HC), bf16),
            pltpu.VMEM((4, Y, 2, RB, HC), bf16),
            pltpu.VMEM((4, RB, HC), bf16),
            pltpu.VMEM((4, RB, HC), bf16),
            pltpu.SemaphoreType.DMA((len(IDS),)),
            pltpu.SemaphoreType.DMA((len(IDS),)),
            pltpu.SemaphoreType.DMA((7,)),
        ],
        compiler_params=pltpu.CompilerParams(collective_id=0, has_side_effects=True),
    )(
        tokens, gain.reshape(64, 128), stale, bias.reshape(1, HC),
        first, second, grad, residual, exponent,
    )
    return (new_first, new_second, out.reshape(256, HC))


def solution(mesh):
    rows = P(("dp", "tensor"), None)
    return jax.shard_map(
        on_device,
        mesh=mesh,
        in_specs=(rows, P(), P(None, "tensor"), P("tensor"), rows, rows, rows, rows, rows),
        out_specs=(rows, rows, P("dp", "tensor")),
        check_vma=False,
    )
```

```python
import jax
import jax.numpy as jnp
from jax import lax
from jax.experimental import pallas as pl
from jax.experimental.pallas import tpu as pltpu
from jax.sharding import PartitionSpec as P

MESH = pl.DeviceIdType.MESH
X, Y, ZL, ZH, C = 4, 4, 4, 2, 2
Z = ZL * ZH
RB = 32
KS = 2048
HC = 256


def ids():
    table = {}

    def add(*key):
        table[key] = len(table)

    add("stale")
    for i in range(1, 4):
        add("y", i)
        add("r", i)
        add("d", i)
    for p in range(4):
        add("xr", p)
        add("xl", p)
    add("fr", 1)
    add("fl", 3)
    for p in (0, 2):
        add("fr", p)
        add("fl", p)
    for h in range(2):
        for d in range(4):
            for cc in range(2 if d < 3 else 1):
                add("z", h, d, cc)
        for d in range(5):
            for cc in range(2 if 0 < d < 4 else 1):
                add("s", h, d, cc)
    for b in range(4):
        add("zx", b)
        for dy in range(1, 4):
            for h in range(2):
                add("c", b, h, dy)
    return table


IDS = ids()


def kernel(
    tok_in, gain_ref, stale_ref, bias_ref, first_in, second_in, grad_in, resid_in, expo_ref,
    out_ref,
    tokv, first_ref, second_ref, grad_ref, resid_ref,
    tok, wbuf, sloc, spart, dsend, drecv, rbuf, rsend, cf, cb, cin, zs, zin, send, recv, loc,
):
    dp = lax.axis_index("dp")
    t = lax.axis_index("tensor")
    c = lax.rem(dp, C)
    y = lax.rem(dp // C, Y)
    zl = dp // (C * Y)
    x = t // ZH
    zh = lax.rem(t, ZH)
    z = zh * ZL + zl

    def at(x_=None, y_=None, z_=None, c_=None):
        x_ = x if x_ is None else x_
        y_ = y if y_ is None else y_
        z_ = z if z_ is None else z_
        c_ = c if c_ is None else c_
        return ((lax.rem(z_, ZL) * Y + y_) * C + c_, x_ * ZH + z_ // ZL)

    xs = [lax.rem(x + i, X) for i in range(X)]
    ys = [lax.rem(y + i, Y) for i in range(Y)]
    zr = [lax.rem(z + i, Z) for i in range(Z)]
    right, left = at(x_=xs[1]), at(x_=xs[3])
    up_z, down_z, sibling = at(z_=zr[1]), at(z_=zr[7]), at(c_=1 - c)
    mirror, partner = at(z_=Z - 1 - z), at(z_=zr[4])

    halves = (1 - zh, zh)

    def copy(src, dst, dev, *key):
        i = IDS[key]
        return pltpu.make_async_remote_copy(
            src_ref=src, dst_ref=dst, send_sem=send.at[i], recv_sem=recv.at[i],
            device_id=dev, device_id_type=MESH,
        )

    sent = []

    def start(src, dst, dev, *key):
        copy(src, dst, dev, *key).start()
        sent.append((dst, dev, key))

    def arrived(ref, *key):
        copy(ref, ref, right, *key).wait_recv()

    barrier = pltpu.get_barrier_semaphore()
    partners = (
        [mirror, at(x_=xs[2]), at(y_=ys[2]), up_z, down_z, right, left]
        + [at(y_=ys[1]), at(y_=ys[3]), sibling]
    )
    for dev in partners:
        pl.semaphore_signal(barrier, inc=1, device_id=dev, device_id_type=MESH)

    loads = []
    for i, (src, dst) in enumerate((
        (first_in, first_ref), (second_in, second_ref), (grad_in, grad_ref),
        (resid_in, resid_ref), (tok_in, tokv),
    )):
        loads.append(pltpu.make_async_copy(src, dst, loc.at[i]))
        loads[-1].start()

    def stale_rows(dp_, xp, zh_):
        return stale_ref.at[pl.ds(pl.multiple_of(dp_ * 256 + xp * 64 + zh_ * RB, RB), RB), :]

    for xp in range(X):
        pltpu.make_async_copy(stale_rows(dp, xp, zh), sloc.at[xp], loc.at[5]).start()

    for load in loads[:4]:
        load.wait()
    for j in range(16):
        cols = slice(j * 128, (j + 1) * 128)
        g = grad_ref[:, cols]
        nf = 0.9 * first_ref[:, cols] + 0.1 * g
        ns = 0.95 * second_ref[:, cols] + 0.05 * g * g
        corrected = 0.02 * nf / (jnp.sqrt(ns) + 1e-08) + resid_ref[:, cols]
        e = jnp.broadcast_to(expo_ref[:, j:j + 1], (RB, 128))
        up = lax.shift_left(jnp.ones_like(e), e).astype(jnp.float32)
        down = lax.shift_left(jnp.ones_like(e), 30 - e).astype(jnp.float32) * (2.0 ** -30)
        q = jnp.clip(corrected * up, -448.0, 448.0).astype(jnp.bfloat16)
        dsend[j // 4, (j // 2) % 2, :, (j % 2) * 128:(j % 2 + 1) * 128] = (
            q.astype(jnp.float32) * down
        ).astype(jnp.bfloat16)

    lane = lax.broadcasted_iota(jnp.int32, (RB, 128), 1)
    row = lax.broadcasted_iota(jnp.int32, (RB, 128), 0)
    gcol = []
    for xp in range(X):
        grow = jnp.broadcast_to(gain_ref[pl.ds(dp * 2 + xp // 2, 1), :], (RB, 128))
        hit = lane == row + (xp % 2) * 64 + zh * RB
        gcol.append(jnp.sum(jnp.where(hit, grow, 0.0), axis=1, keepdims=True))

    loads[4].wait()
    total = jnp.zeros((RB, 1), jnp.float32)
    for k in range(8):
        v = tokv[:, k * 1024:(k + 1) * 1024].astype(jnp.float32)
        total = total + jnp.sum(v * v, axis=1, keepdims=True)
    rsend[...] = jnp.broadcast_to(lax.rsqrt(total / 8192.0 + 1e-06), (RB, 128))

    pl.semaphore_wait(barrier, len(partners))

    for dx in (1, 3, 2):
        start(dsend.at[xs[dx]], drecv.at[dx], at(x_=xs[dx]), "d", dx)
    dp_m = ((ZL - 1 - zl) * Y + y) * C + c
    for xp in range(X):
        copy(stale_rows(dp_m, xp, 1 - zh), spart.at[xp], mirror, "stale").start()
    sent.append((spart, mirror, ("stale",)))

    def part(k, y_):
        return tokv.at[:, pl.ds(pl.multiple_of(k * 2048 + y_ * 512, 512), 512)]

    def spread(dev, y_, *key):
        for k in range(ZL):
            copy(part(k, y_), tok.at[x, y, :, pl.ds(k * 512, 512)], dev, *key).start()
        sent.append((tok.at[x, y], dev, key))

    spread(at(y_=ys[1]), ys[1], "y", 1)
    spread(at(y_=ys[3]), ys[3], "y", 3)
    spread(right, y, "xr", 0)
    spread(left, y, "xl", 0)
    spread(at(y_=ys[2]), ys[2], "y", 2)
    for k in range(ZL):
        pltpu.make_async_copy(part(k, y), tok.at[x, y, :, pl.ds(k * 512, 512)], loc.at[6]).start()
    for dx in range(1, 4):
        start(rsend, rbuf.at[dx], at(x_=xs[dx]), "r", dx)

    def merge(dx, half, stale):
        xp = xs[(4 - dx) % 4]
        d = dsend[xp, half] if dx == 0 else drecv[dx, half]
        g = gcol[3]
        for i in range(3):
            g = jnp.where(xp == i, gcol[i], g)
        w = g * (stale[xp].astype(jnp.float32) + d.astype(jnp.float32))
        wbuf[zl, c, xp, zh, half] = w.astype(jnp.bfloat16)

    way = 1 - 2 * c
    onward = at(z_=lax.rem(z + way + Z, Z))

    def block(hops, core, h):
        z_ = lax.rem(z + way * hops + 2 * Z, Z)
        return wbuf.at[lax.rem(z_, ZL), core, :, z_ // ZL, h]

    def first_hop(h):
        ref = block(0, c, h)
        start(ref, ref, sibling, "s", h, 0, 0)
        start(ref, ref, onward, "z", h, 0, 0)

    def first_hop_sibling(h):
        ref = block(0, 1 - c, h)
        arrived(ref, "s", h, 0, 0)
        start(ref, ref, onward, "z", h, 0, 1)

    pltpu.make_async_copy(sloc, sloc, loc.at[5]).wait()
    merge(0, zh, sloc)
    for dx in (1, 3, 2):
        arrived(drecv.at[dx], "d", dx)
        merge(dx, zh, sloc)
    arrived(spart, "stale")
    for dx in (0, 1, 3, 2):
        merge(dx, 1 - zh, spart)
    first_hop(0)
    first_hop(1)
    first_hop_sibling(0)
    first_hop_sibling(1)

    def from_y(p):
        ref = tok.at[x, ys[(4 - p) % 4]]
        arrived(ref, "y", p)
        start(ref, ref, right, "xr", p)
        start(ref, ref, left, "xl", p)

    def token(i, p, rows=None):
        ref = tok.at[xs[i], ys[(4 - p) % 4]]
        return ref if rows is None else ref.at[pl.ds(rows, RB // 2), :]

    def ring(d):
        for cc in range(2 if d < 4 else 1):
            for h in range(2):
                ref = block(-d, 1 - c if cc else c, h)
                arrived(ref, "z", h, d - 1, cc)
                if d < 3 or (d == 3 and cc == 0):
                    start(ref, ref, onward, "z", h, d, cc)
                start(ref, ref, sibling, "s", h, d, cc)

    def forward(p):
        if p == 1:
            arrived(token(3, 1), "xr", 1)
            start(token(3, 1), token(3, 1), right, "fr", 1)
            arrived(token(1, 3), "xl", 3)
            start(token(1, 3), token(1, 3), left, "fl", 3)
        else:
            arrived(token(3, p), "xr", p)
            start(token(3, p, 0), token(3, p, 0), right, "fr", p)
            arrived(token(1, p), "xl", p)
            start(token(1, p, 16), token(1, p, 16), left, "fl", p)

    def siblings(d):
        for cc in range(2 if d < 4 else 1):
            for h in range(2):
                arrived(block(d, c if cc else 1 - c, h), "s", h, d, cc)

    def weights(k):
        return wbuf[:, :, :, :, halves[k]].reshape(KS, HC)

    def send_partial(b, h):
        for dy in (1, 3, 2):
            start(cb.at[b, h, ys[dy]], cin.at[b, h, dy], at(y_=ys[dy]), "c", b, h, dy)

    def product(b, h):
        a = tok[order[b]].reshape(Y * RB, KS)
        acc = jnp.dot(a, weights(h), preferred_element_type=jnp.float32)
        acc = acc.reshape(Y, RB, HC)
        cf[b, h] = acc
        cb[b, h] = acc.astype(jnp.bfloat16)
        send_partial(b, h)

    def product_far(h):
        a = jnp.concatenate([tok[xs[2], ys[dy]] for dy in (1, 2, 3)], axis=0)
        acc = jnp.dot(a, weights(h), preferred_element_type=jnp.float32)
        for i, dy in enumerate((1, 2, 3)):
            cb[3, h, ys[dy]] = acc[i * RB:(i + 1) * RB].astype(jnp.bfloat16)
        send_partial(3, h)

    def product_last(k):
        cf[3, k, y] = jnp.dot(tok[xs[2], y], weights(k), preferred_element_type=jnp.float32)

    order = (x, xs[3], xs[1], xs[2])

    def total_of(b, k):
        for dy in (1, 3, 2):
            arrived(cin.at[b, k, dy], "c", b, k, dy)
        v = cf[b, k, y]
        for dy in range(1, 4):
            v = v + cin[b, k, dy].astype(jnp.float32)
        dx = (0, 1, 3, 2)[b]
        return v * (rbuf[dx, :, :1] if b else rsend[:, :1])

    def finish(b, k):
        if k == 0:
            if b:
                dx = (0, 1, 3, 2)[b]
                arrived(rbuf.at[dx], "r", dx)
            zs[b] = total_of(b, 0).astype(jnp.bfloat16)
            start(zs.at[b], zin.at[b], partner, "zx", b)
        else:
            out_ref[order[b] * 2 + zh] = (total_of(b, 1) + bias_ref[...]).astype(jnp.bfloat16)

    def own_tokens():
        pltpu.make_async_copy(tok.at[x, y], tok.at[x, y], loc.at[6]).wait()

    def near_tokens():
        arrived(token(3, 3), "xr", 3)
        arrived(token(1, 1), "xl", 1)

    def far_tokens():
        arrived(token(2, 1), "fr", 1)
        arrived(token(2, 3), "fl", 3)
        arrived(token(2, 2, 0), "fr", 2)
        arrived(token(2, 2, 16), "fl", 2)

    def last_tokens():
        arrived(token(2, 0, 0), "fr", 0)
        arrived(token(2, 0, 16), "fl", 0)

    from_y(1)
    from_y(3)
    ring(1)
    from_y(2)
    ring(2)
    forward(1)
    ring(3)
    forward(2)
    forward(0)
    ring(4)
    own_tokens()
    for d in range(1, 5):
        siblings(d)
    product(0, 0)
    near_tokens()
    product(1, 0)
    product(2, 0)
    far_tokens()
    product_far(0)
    for b in range(3):
        product(b, 1)
    product_far(1)
    for b in range(3):
        finish(b, 0)
    last_tokens()
    product_last(0)
    finish(3, 0)
    product_last(1)
    for b in range(4):
        finish(b, 1)
    for b in range(4):
        arrived(zin.at[b], "zx", b)
        out_ref[order[b] * 2 + 1 - zh] = (
            zin[b].astype(jnp.float32) + bias_ref[...]
        ).astype(jnp.bfloat16)
    for dst, dev, key in sent:
        copy(dst, dst, dev, *key).wait_send()


def on_device(tokens, gain, stale, bias, first, second, grad, residual, exponent):
    new_first = 0.9 * first + 0.1 * grad
    new_second = 0.95 * second + 0.05 * grad * grad
    vmem = pl.BlockSpec(memory_space=pltpu.VMEM)
    there = pl.BlockSpec(memory_space=pl.ANY)
    bf16, f32 = jnp.bfloat16, jnp.float32
    out = pl.pallas_call(
        kernel,
        out_shape=jax.ShapeDtypeStruct((8, RB, HC), bf16),
        in_specs=[there, vmem, there, vmem, there, there, there, there, vmem],
        out_specs=vmem,
        scratch_shapes=[
            pltpu.VMEM((RB, 8192), bf16),
            pltpu.VMEM((RB, 2048), f32),
            pltpu.VMEM((RB, 2048), f32),
            pltpu.VMEM((RB, 2048), f32),
            pltpu.VMEM((RB, 2048), f32),
            pltpu.VMEM((X, Y, RB, KS), bf16),
            pltpu.VMEM((ZL, C, X, ZH, 2, RB, HC), bf16),
            pltpu.VMEM((X, RB, HC), bf16),
            pltpu.VMEM((X, RB, HC), bf16),
            pltpu.VMEM((X, 2, RB, HC), bf16),
            pltpu.VMEM((X, 2, RB, HC), bf16),
            pltpu.VMEM((X, RB, 128), f32),
            pltpu.VMEM((RB, 128), f32),
            pltpu.VMEM((4, 2, Y, RB, HC), f32),
            pltpu.VMEM((4, 2, Y, RB, HC), bf16),
            pltpu.VMEM((4, 2, Y, RB, HC), bf16),
            pltpu.VMEM((4, RB, HC), bf16),
            pltpu.VMEM((4, RB, HC), bf16),
            pltpu.SemaphoreType.DMA((len(IDS),)),
            pltpu.SemaphoreType.DMA((len(IDS),)),
            pltpu.SemaphoreType.DMA((7,)),
        ],
        compiler_params=pltpu.CompilerParams(collective_id=0, has_side_effects=True),
    )(
        tokens, gain.reshape(64, 128), stale, bias.reshape(1, HC),
        first, second, grad, residual, exponent,
    )
    return (new_first, new_second, out.reshape(256, HC))


def solution(mesh):
    rows = P(("dp", "tensor"), None)
    return jax.shard_map(
        on_device,
        mesh=mesh,
        in_specs=(rows, P(), P(None, "tensor"), P("tensor"), rows, rows, rows, rows, rows),
        out_specs=(rows, rows, P("dp", "tensor")),
        check_vma=False,
    )
```

```python
import jax
import jax.numpy as jnp
from jax import lax
from jax.experimental import pallas as pl
from jax.experimental.pallas import tpu as pltpu
from jax.sharding import PartitionSpec as P

MESH = pl.DeviceIdType.MESH
X, Y, ZL, ZH, C = 4, 4, 4, 2, 2
Z = ZL * ZH
RB = 32
KS = 2048
HC = 256


def ids():
    table = {}

    def add(*key):
        table[key] = len(table)

    add("stale")
    for i in range(1, 4):
        add("y", i)
        add("r", i)
        add("d", i)
    for p in range(4):
        add("xr", p)
        add("xl", p)
    add("fr", 1)
    add("fl", 3)
    for p in (0, 2):
        add("fr", p)
        add("fl", p)
    for h in range(2):
        for d in range(4):
            for cc in range(2 if d < 3 else 1):
                add("z", h, d, cc)
        for d in range(5):
            for cc in range(2 if 0 < d < 4 else 1):
                add("s", h, d, cc)
    for b in range(4):
        add("zx", b)
        for dy in range(1, 4):
            for h in range(2):
                add("c", b, h, dy)
    return table


IDS = ids()


def kernel(
    tok_in, gain_ref, stale_ref, bias_ref, first_in, second_in, grad_in, resid_in, expo_ref,
    out_ref,
    tokv, first_ref, second_ref, grad_ref, resid_ref,
    tok, wbuf, sloc, spart, dsend, drecv, rbuf, rsend, cf, cb, cin, zs, zin, send, recv, loc,
):
    dp = lax.axis_index("dp")
    t = lax.axis_index("tensor")
    c = lax.rem(dp, C)
    y = lax.rem(dp // C, Y)
    zl = dp // (C * Y)
    x = t // ZH
    zh = lax.rem(t, ZH)
    z = zh * ZL + zl

    def at(x_=None, y_=None, z_=None, c_=None):
        x_ = x if x_ is None else x_
        y_ = y if y_ is None else y_
        z_ = z if z_ is None else z_
        c_ = c if c_ is None else c_
        return ((lax.rem(z_, ZL) * Y + y_) * C + c_, x_ * ZH + z_ // ZL)

    xs = [lax.rem(x + i, X) for i in range(X)]
    ys = [lax.rem(y + i, Y) for i in range(Y)]
    zr = [lax.rem(z + i, Z) for i in range(Z)]
    right, left = at(x_=xs[1]), at(x_=xs[3])
    up_z, down_z, sibling = at(z_=zr[1]), at(z_=zr[7]), at(c_=1 - c)
    mirror, partner = at(z_=Z - 1 - z), at(z_=zr[4])

    halves = (1 - zh, zh)

    def copy(src, dst, dev, *key):
        i = IDS[key]
        return pltpu.make_async_remote_copy(
            src_ref=src, dst_ref=dst, send_sem=send.at[i], recv_sem=recv.at[i],
            device_id=dev, device_id_type=MESH,
        )

    sent = []

    def start(src, dst, dev, *key):
        copy(src, dst, dev, *key).start()
        sent.append((dst, dev, key))

    def arrived(ref, *key):
        copy(ref, ref, right, *key).wait_recv()

    barrier = pltpu.get_barrier_semaphore()
    partners = (
        [mirror, at(x_=xs[2]), at(y_=ys[2]), up_z, down_z, right, left]
        + [at(y_=ys[1]), at(y_=ys[3]), sibling]
    )
    for dev in partners:
        pl.semaphore_signal(barrier, inc=1, device_id=dev, device_id_type=MESH)

    loads = []
    for i, (src, dst) in enumerate((
        (first_in, first_ref), (second_in, second_ref), (grad_in, grad_ref),
        (resid_in, resid_ref), (tok_in, tokv),
    )):
        loads.append(pltpu.make_async_copy(src, dst, loc.at[i]))
        loads[-1].start()

    def stale_rows(dp_, xp, zh_):
        return stale_ref.at[pl.ds(pl.multiple_of(dp_ * 256 + xp * 64 + zh_ * RB, RB), RB), :]

    for xp in range(X):
        pltpu.make_async_copy(stale_rows(dp, xp, zh), sloc.at[xp], loc.at[5]).start()

    for load in loads[:4]:
        load.wait()
    for j in range(16):
        cols = slice(j * 128, (j + 1) * 128)
        g = grad_ref[:, cols]
        nf = 0.9 * first_ref[:, cols] + 0.1 * g
        ns = 0.95 * second_ref[:, cols] + 0.05 * g * g
        corrected = 0.02 * nf / (jnp.sqrt(ns) + 1e-08) + resid_ref[:, cols]
        e = jnp.broadcast_to(expo_ref[:, j:j + 1], (RB, 128))
        up = lax.shift_left(jnp.ones_like(e), e).astype(jnp.float32)
        down = lax.shift_left(jnp.ones_like(e), 30 - e).astype(jnp.float32) * (2.0 ** -30)
        q = jnp.clip(corrected * up, -448.0, 448.0).astype(jnp.bfloat16)
        dsend[j // 4, (j // 2) % 2, :, (j % 2) * 128:(j % 2 + 1) * 128] = (
            q.astype(jnp.float32) * down
        ).astype(jnp.bfloat16)

    lane = lax.broadcasted_iota(jnp.int32, (RB, 128), 1)
    row = lax.broadcasted_iota(jnp.int32, (RB, 128), 0)
    gcol = []
    for xp in range(X):
        grow = jnp.broadcast_to(gain_ref[pl.ds(dp * 2 + xp // 2, 1), :], (RB, 128))
        hit = lane == row + (xp % 2) * 64 + zh * RB
        gcol.append(jnp.sum(jnp.where(hit, grow, 0.0), axis=1, keepdims=True))

    loads[4].wait()
    total = jnp.zeros((RB, 1), jnp.float32)
    for k in range(8):
        v = tokv[:, k * 1024:(k + 1) * 1024].astype(jnp.float32)
        total = total + jnp.sum(v * v, axis=1, keepdims=True)
    rsend[...] = jnp.broadcast_to(lax.rsqrt(total / 8192.0 + 1e-06), (RB, 128))

    pl.semaphore_wait(barrier, len(partners))

    for dx in (1, 3, 2):
        start(dsend.at[xs[dx]], drecv.at[dx], at(x_=xs[dx]), "d", dx)
    dp_m = ((ZL - 1 - zl) * Y + y) * C + c
    for xp in range(X):
        copy(stale_rows(dp_m, xp, 1 - zh), spart.at[xp], mirror, "stale").start()
    sent.append((spart, mirror, ("stale",)))

    def part(k, y_):
        return tokv.at[:, pl.ds(pl.multiple_of(k * 2048 + y_ * 512, 512), 512)]

    def spread(dev, y_, *key):
        for k in range(ZL):
            copy(part(k, y_), tok.at[x, y, :, pl.ds(k * 512, 512)], dev, *key).start()
        sent.append((tok.at[x, y], dev, key))

    spread(at(y_=ys[1]), ys[1], "y", 1)
    spread(at(y_=ys[3]), ys[3], "y", 3)
    spread(right, y, "xr", 0)
    spread(left, y, "xl", 0)
    spread(at(y_=ys[2]), ys[2], "y", 2)
    for k in range(ZL):
        pltpu.make_async_copy(part(k, y), tok.at[x, y, :, pl.ds(k * 512, 512)], loc.at[6]).start()
    for dx in range(1, 4):
        start(rsend, rbuf.at[dx], at(x_=xs[dx]), "r", dx)

    def merge(dx, half, stale):
        xp = xs[(4 - dx) % 4]
        d = dsend[xp, half] if dx == 0 else drecv[dx, half]
        g = gcol[3]
        for i in range(3):
            g = jnp.where(xp == i, gcol[i], g)
        w = g * (stale[xp].astype(jnp.float32) + d.astype(jnp.float32))
        wbuf[zl, c, xp, zh, half] = w.astype(jnp.bfloat16)

    way = 1 - 2 * c
    onward = at(z_=lax.rem(z + way + Z, Z))

    def block(hops, core, h):
        z_ = lax.rem(z + way * hops + 2 * Z, Z)
        return wbuf.at[lax.rem(z_, ZL), core, :, z_ // ZL, h]

    def first_hop(h):
        ref = block(0, c, h)
        start(ref, ref, sibling, "s", h, 0, 0)
        start(ref, ref, onward, "z", h, 0, 0)

    def first_hop_sibling(h):
        ref = block(0, 1 - c, h)
        arrived(ref, "s", h, 0, 0)
        start(ref, ref, onward, "z", h, 0, 1)

    pltpu.make_async_copy(sloc, sloc, loc.at[5]).wait()
    merge(0, zh, sloc)
    for dx in (1, 3, 2):
        arrived(drecv.at[dx], "d", dx)
        merge(dx, zh, sloc)
    arrived(spart, "stale")
    for dx in (0, 1, 3, 2):
        merge(dx, 1 - zh, spart)
    first_hop(0)
    first_hop(1)
    first_hop_sibling(0)
    first_hop_sibling(1)

    def from_y(p):
        ref = tok.at[x, ys[(4 - p) % 4]]
        arrived(ref, "y", p)
        start(ref, ref, right, "xr", p)
        start(ref, ref, left, "xl", p)

    def token(i, p, rows=None):
        ref = tok.at[xs[i], ys[(4 - p) % 4]]
        return ref if rows is None else ref.at[pl.ds(rows, RB // 2), :]

    def ring(d):
        for cc in range(2 if d < 4 else 1):
            for h in range(2):
                ref = block(-d, 1 - c if cc else c, h)
                arrived(ref, "z", h, d - 1, cc)
                if d < 3 or (d == 3 and cc == 0):
                    start(ref, ref, onward, "z", h, d, cc)
                start(ref, ref, sibling, "s", h, d, cc)

    def forward(p):
        if p == 1:
            arrived(token(3, 1), "xr", 1)
            start(token(3, 1), token(3, 1), right, "fr", 1)
            arrived(token(1, 3), "xl", 3)
            start(token(1, 3), token(1, 3), left, "fl", 3)
        else:
            arrived(token(3, p), "xr", p)
            start(token(3, p, 0), token(3, p, 0), right, "fr", p)
            arrived(token(1, p), "xl", p)
            start(token(1, p, 16), token(1, p, 16), left, "fl", p)

    def siblings(d):
        for cc in range(2 if d < 4 else 1):
            for h in range(2):
                arrived(block(d, c if cc else 1 - c, h), "s", h, d, cc)

    def weights(k):
        return wbuf[:, :, :, :, halves[k]].reshape(KS, HC)

    def send_partial(b, h):
        for dy in (1, 3, 2):
            start(cb.at[b, h, ys[dy]], cin.at[b, h, dy], at(y_=ys[dy]), "c", b, h, dy)

    def product(b, h):
        a = tok[order[b]].reshape(Y * RB, KS)
        acc = jnp.dot(a, weights(h), preferred_element_type=jnp.float32)
        acc = acc.reshape(Y, RB, HC)
        cf[b, h] = acc
        cb[b, h] = acc.astype(jnp.bfloat16)
        send_partial(b, h)

    def product_far(h):
        a = jnp.concatenate([tok[xs[2], ys[dy]] for dy in (1, 2, 3)], axis=0)
        acc = jnp.dot(a, weights(h), preferred_element_type=jnp.float32)
        for i, dy in enumerate((1, 2, 3)):
            cb[3, h, ys[dy]] = acc[i * RB:(i + 1) * RB].astype(jnp.bfloat16)
        send_partial(3, h)

    def product_last(k):
        cf[3, k, y] = jnp.dot(tok[xs[2], y], weights(k), preferred_element_type=jnp.float32)

    order = (x, xs[3], xs[1], xs[2])

    def total_of(b, k):
        for dy in (1, 3, 2):
            arrived(cin.at[b, k, dy], "c", b, k, dy)
        v = cf[b, k, y]
        for dy in range(1, 4):
            v = v + cin[b, k, dy].astype(jnp.float32)
        dx = (0, 1, 3, 2)[b]
        return v * (rbuf[dx, :, :1] if b else rsend[:, :1])

    def finish(b, k):
        if k == 0:
            if b:
                dx = (0, 1, 3, 2)[b]
                arrived(rbuf.at[dx], "r", dx)
            zs[b] = total_of(b, 0).astype(jnp.bfloat16)
            start(zs.at[b], zin.at[b], partner, "zx", b)
        else:
            out_ref[order[b] * 2 + zh] = (total_of(b, 1) + bias_ref[...]).astype(jnp.bfloat16)

    def own_tokens():
        pltpu.make_async_copy(tok.at[x, y], tok.at[x, y], loc.at[6]).wait()

    def near_tokens():
        arrived(token(3, 3), "xr", 3)
        arrived(token(1, 1), "xl", 1)

    def far_tokens():
        arrived(token(2, 1), "fr", 1)
        arrived(token(2, 3), "fl", 3)
        arrived(token(2, 2, 0), "fr", 2)
        arrived(token(2, 2, 16), "fl", 2)

    def last_tokens():
        arrived(token(2, 0, 0), "fr", 0)
        arrived(token(2, 0, 16), "fl", 0)

    from_y(1)
    from_y(3)
    ring(1)
    from_y(2)
    ring(2)
    forward(1)
    ring(3)
    forward(2)
    forward(0)
    ring(4)
    own_tokens()
    for d in range(1, 5):
        siblings(d)
    product(0, 0)
    near_tokens()
    product(1, 0)
    product(2, 0)
    far_tokens()
    product_far(0)
    for b in range(3):
        product(b, 1)
    product_far(1)
    for b in range(3):
        finish(b, 0)
    last_tokens()
    product_last(0)
    finish(3, 0)
    product_last(1)
    for b in range(4):
        finish(b, 1)
    for b in range(4):
        arrived(zin.at[b], "zx", b)
        out_ref[order[b] * 2 + 1 - zh] = (
            zin[b].astype(jnp.float32) + bias_ref[...]
        ).astype(jnp.bfloat16)
    for dst, dev, key in sent:
        copy(dst, dst, dev, *key).wait_send()


def on_device(tokens, gain, stale, bias, first, second, grad, residual, exponent):
    new_first = 0.9 * first + 0.1 * grad
    new_second = 0.95 * second + 0.05 * grad * grad
    vmem = pl.BlockSpec(memory_space=pltpu.VMEM)
    there = pl.BlockSpec(memory_space=pl.ANY)
    bf16, f32 = jnp.bfloat16, jnp.float32
    out = pl.pallas_call(
        kernel,
        out_shape=pltpu.VMEM((8, RB, HC), bf16),
        in_specs=[there, vmem, there, vmem, there, there, there, there, vmem],
        out_specs=vmem,
        scratch_shapes=[
            pltpu.VMEM((RB, 8192), bf16),
            pltpu.VMEM((RB, 2048), f32),
            pltpu.VMEM((RB, 2048), f32),
            pltpu.VMEM((RB, 2048), f32),
            pltpu.VMEM((RB, 2048), f32),
            pltpu.VMEM((X, Y, RB, KS), bf16),
            pltpu.VMEM((ZL, C, X, ZH, 2, RB, HC), bf16),
            pltpu.VMEM((X, RB, HC), bf16),
            pltpu.VMEM((X, RB, HC), bf16),
            pltpu.VMEM((X, 2, RB, HC), bf16),
            pltpu.VMEM((X, 2, RB, HC), bf16),
            pltpu.VMEM((X, RB, 128), f32),
            pltpu.VMEM((RB, 128), f32),
            pltpu.VMEM((4, 2, Y, RB, HC), f32),
            pltpu.VMEM((4, 2, Y, RB, HC), bf16),
            pltpu.VMEM((4, 2, Y, RB, HC), bf16),
            pltpu.VMEM((4, RB, HC), bf16),
            pltpu.VMEM((4, RB, HC), bf16),
            pltpu.SemaphoreType.DMA((len(IDS),)),
            pltpu.SemaphoreType.DMA((len(IDS),)),
            pltpu.SemaphoreType.DMA((7,)),
        ],
        compiler_params=pltpu.CompilerParams(collective_id=0, has_side_effects=True),
    )(
        tokens, gain.reshape(64, 128), stale, bias.reshape(1, HC),
        first, second, grad, residual, exponent,
    )
    return (new_first, new_second, out.reshape(256, HC))


def solution(mesh):
    rows = P(("dp", "tensor"), None)
    return jax.shard_map(
        on_device,
        mesh=mesh,
        in_specs=(rows, P(), P(None, "tensor"), P("tensor"), rows, rows, rows, rows, rows),
        out_specs=(rows, rows, P("dp", "tensor")),
        check_vma=False,
    )
```

```python
import jax
import jax.numpy as jnp
from jax import lax
from jax.experimental import pallas as pl
from jax.experimental.pallas import tpu as pltpu
from jax.sharding import PartitionSpec as P

MESH = pl.DeviceIdType.MESH
X, Y, ZL, ZH, C = 4, 4, 4, 2, 2
Z = ZL * ZH
RB = 32
KS = 2048
HC = 256


def ids():
    table = {}

    def add(*key):
        table[key] = len(table)

    add("stale")
    for i in range(1, 4):
        add("y", i)
        add("r", i)
        add("d", i)
    for p in range(4):
        add("xr", p)
        add("xl", p)
    add("fr", 1)
    add("fl", 3)
    for p in (0, 2):
        add("fr", p)
        add("fl", p)
    for h in range(2):
        for d in range(4):
            for cc in range(2 if d < 3 else 1):
                add("z", h, d, cc)
        for d in range(5):
            for cc in range(2 if 0 < d < 4 else 1):
                add("s", h, d, cc)
    for b in range(4):
        add("zx", b)
        for dy in range(1, 4):
            for h in range(2):
                add("c", b, h, dy)
    return table


IDS = ids()


def kernel(
    tok_in, gain_ref, stale_ref, bias_ref, first_in, second_in, grad_in, resid_in, expo_ref,
    out_ref,
    tokv, first_ref, second_ref, grad_ref, resid_ref,
    tok, wbuf, sloc, spart, dsend, drecv, rbuf, rsend, cf, cb, cin, zs, zin, send, recv, loc,
):
    dp = lax.axis_index("dp")
    t = lax.axis_index("tensor")
    c = lax.rem(dp, C)
    y = lax.rem(dp // C, Y)
    zl = dp // (C * Y)
    x = t // ZH
    zh = lax.rem(t, ZH)
    z = zh * ZL + zl

    def at(x_=None, y_=None, z_=None, c_=None):
        x_ = x if x_ is None else x_
        y_ = y if y_ is None else y_
        z_ = z if z_ is None else z_
        c_ = c if c_ is None else c_
        return ((lax.rem(z_, ZL) * Y + y_) * C + c_, x_ * ZH + z_ // ZL)

    xs = [lax.rem(x + i, X) for i in range(X)]
    ys = [lax.rem(y + i, Y) for i in range(Y)]
    zr = [lax.rem(z + i, Z) for i in range(Z)]
    right, left = at(x_=xs[1]), at(x_=xs[3])
    up_z, down_z, sibling = at(z_=zr[1]), at(z_=zr[7]), at(c_=1 - c)
    mirror, partner = at(z_=Z - 1 - z), at(z_=zr[4])

    halves = (1 - zh, zh)

    def copy(src, dst, dev, *key):
        i = IDS[key]
        return pltpu.make_async_remote_copy(
            src_ref=src, dst_ref=dst, send_sem=send.at[i], recv_sem=recv.at[i],
            device_id=dev, device_id_type=MESH,
        )

    sent = []

    def start(src, dst, dev, *key):
        copy(src, dst, dev, *key).start()
        sent.append((dst, dev, key))

    def arrived(ref, *key):
        copy(ref, ref, right, *key).wait_recv()

    barrier = pltpu.get_barrier_semaphore()
    partners = (
        [mirror, at(x_=xs[2]), at(y_=ys[2]), up_z, down_z, right, left]
        + [at(y_=ys[1]), at(y_=ys[3]), sibling]
    )
    for dev in partners:
        pl.semaphore_signal(barrier, inc=1, device_id=dev, device_id_type=MESH)

    loads = []
    for i, (src, dst) in enumerate((
        (first_in, first_ref), (second_in, second_ref), (grad_in, grad_ref),
        (resid_in, resid_ref), (tok_in, tokv),
    )):
        loads.append(pltpu.make_async_copy(src, dst, loc.at[i]))
        loads[-1].start()

    def stale_rows(dp_, xp, zh_):
        return stale_ref.at[pl.ds(pl.multiple_of(dp_ * 256 + xp * 64 + zh_ * RB, RB), RB), :]

    for xp in range(X):
        pltpu.make_async_copy(stale_rows(dp, xp, zh), sloc.at[xp], loc.at[5]).start()

    for load in loads[:4]:
        load.wait()
    for j in range(16):
        cols = slice(j * 128, (j + 1) * 128)
        g = grad_ref[:, cols]
        nf = 0.9 * first_ref[:, cols] + 0.1 * g
        ns = 0.95 * second_ref[:, cols] + 0.05 * g * g
        corrected = 0.02 * nf / (jnp.sqrt(ns) + 1e-08) + resid_ref[:, cols]
        e = jnp.broadcast_to(expo_ref[:, j:j + 1], (RB, 128))
        up = lax.shift_left(jnp.ones_like(e), e).astype(jnp.float32)
        down = lax.shift_left(jnp.ones_like(e), 30 - e).astype(jnp.float32) * (2.0 ** -30)
        q = jnp.clip(corrected * up, -448.0, 448.0).astype(jnp.bfloat16)
        dsend[j // 4, (j // 2) % 2, :, (j % 2) * 128:(j % 2 + 1) * 128] = (
            q.astype(jnp.float32) * down
        ).astype(jnp.bfloat16)

    lane = lax.broadcasted_iota(jnp.int32, (RB, 128), 1)
    row = lax.broadcasted_iota(jnp.int32, (RB, 128), 0)
    gcol = []
    for xp in range(X):
        grow = jnp.broadcast_to(gain_ref[pl.ds(dp * 2 + xp // 2, 1), :], (RB, 128))
        hit = lane == row + (xp % 2) * 64 + zh * RB
        gcol.append(jnp.sum(jnp.where(hit, grow, 0.0), axis=1, keepdims=True))

    loads[4].wait()
    total = jnp.zeros((RB, 1), jnp.float32)
    for k in range(8):
        v = tokv[:, k * 1024:(k + 1) * 1024].astype(jnp.float32)
        total = total + jnp.sum(v * v, axis=1, keepdims=True)
    scale = lax.rsqrt(total / 8192.0 + 1e-06)
    rsend[...] = jnp.broadcast_to(
        jnp.sum(jnp.where(lane == row, scale, 0.0), axis=0, keepdims=True), (8, 128)
    )

    pl.semaphore_wait(barrier, len(partners))

    for dx in (1, 3, 2):
        start(dsend.at[xs[dx]], drecv.at[dx], at(x_=xs[dx]), "d", dx)
    dp_m = ((ZL - 1 - zl) * Y + y) * C + c
    for xp in range(X):
        copy(stale_rows(dp_m, xp, 1 - zh), spart.at[xp], mirror, "stale").start()
    sent.append((spart, mirror, ("stale",)))

    def part(k, y_):
        return tokv.at[:, pl.ds(pl.multiple_of(k * 2048 + y_ * 512, 512), 512)]

    def spread(dev, y_, *key):
        for k in range(ZL):
            copy(part(k, y_), tok.at[x, y, :, pl.ds(k * 512, 512)], dev, *key).start()
        sent.append((tok.at[x, y], dev, key))

    spread(at(y_=ys[1]), ys[1], "y", 1)
    spread(at(y_=ys[3]), ys[3], "y", 3)
    spread(right, y, "xr", 0)
    spread(left, y, "xl", 0)
    spread(at(y_=ys[2]), ys[2], "y", 2)
    for k in range(ZL):
        pltpu.make_async_copy(part(k, y), tok.at[x, y, :, pl.ds(k * 512, 512)], loc.at[6]).start()
    for dx in range(1, 4):
        start(rsend, rbuf.at[dx], at(x_=xs[dx]), "r", dx)

    def merge(dx, half, stale):
        xp = xs[(4 - dx) % 4]
        d = dsend[xp, half] if dx == 0 else drecv[dx, half]
        g = gcol[3]
        for i in range(3):
            g = jnp.where(xp == i, gcol[i], g)
        w = g * (stale[xp].astype(jnp.float32) + d.astype(jnp.float32))
        wbuf[zl, c, xp, zh, half] = w.astype(jnp.bfloat16)

    way = 1 - 2 * c
    onward = at(z_=lax.rem(z + way + Z, Z))

    def block(hops, core, h):
        z_ = lax.rem(z + way * hops + 2 * Z, Z)
        zh_ = z_ // ZL
        return wbuf.at[lax.rem(z_, ZL), core, :, zh_, 1 - zh_ if h else zh_]

    def first_hop(h):
        ref = block(0, c, h)
        start(ref, ref, sibling, "s", h, 0, 0)
        start(ref, ref, onward, "z", h, 0, 0)

    def first_hop_sibling(h):
        ref = block(0, 1 - c, h)
        arrived(ref, "s", h, 0, 0)
        start(ref, ref, onward, "z", h, 0, 1)

    pltpu.make_async_copy(sloc, sloc, loc.at[5]).wait()
    merge(0, zh, sloc)
    for dx in (1, 3, 2):
        arrived(drecv.at[dx], "d", dx)
        merge(dx, zh, sloc)
    first_hop(0)
    arrived(spart, "stale")
    for dx in (0, 1, 3, 2):
        merge(dx, 1 - zh, spart)
    first_hop(1)

    def from_y(p):
        ref = tok.at[x, ys[(4 - p) % 4]]
        arrived(ref, "y", p)
        start(ref, ref, right, "xr", p)
        start(ref, ref, left, "xl", p)

    def token(i, p, rows=None):
        ref = tok.at[xs[i], ys[(4 - p) % 4]]
        return ref if rows is None else ref.at[pl.ds(rows, RB // 2), :]

    def ring(d, hs=(0, 1)):
        for cc in range(2 if d < 4 else 1):
            for h in hs:
                ref = block(-d, 1 - c if cc else c, h)
                arrived(ref, "z", h, d - 1, cc)
                if d < 3 or (d == 3 and cc == 0):
                    start(ref, ref, onward, "z", h, d, cc)
                start(ref, ref, sibling, "s", h, d, cc)

    def forward(p):
        if p == 1:
            arrived(token(3, 1), "xr", 1)
            start(token(3, 1), token(3, 1), right, "fr", 1)
            arrived(token(1, 3), "xl", 3)
            start(token(1, 3), token(1, 3), left, "fl", 3)
        else:
            arrived(token(3, p), "xr", p)
            start(token(3, p, 0), token(3, p, 0), right, "fr", p)
            arrived(token(1, p), "xl", p)
            start(token(1, p, 16), token(1, p, 16), left, "fl", p)

    def siblings(d, hs=(0, 1)):
        for cc in range(2 if d < 4 else 1):
            for h in hs:
                arrived(block(d, c if cc else 1 - c, h), "s", h, d, cc)

    def quarter(i, k):
        return wbuf[zls[i], :, :, :, halves[k]].reshape(KS // ZL, HC)

    zls = [lax.rem(zl + i, ZL) for i in range(ZL)]

    def columns(i):
        return pl.ds(pl.multiple_of(zls[i] * 512, 512), 512)

    def partial(a_of, ks, k):
        acc = None
        for i in ks:
            one = jnp.dot(a_of(i), quarter(i, k), preferred_element_type=jnp.float32)
            acc = one if acc is None else acc + one
        return acc

    def send_partial(b, h):
        for dy in (1, 3, 2):
            start(cb.at[b, h, ys[dy]], cin.at[b, h, dy], at(y_=ys[dy]), "c", b, h, dy)

    def rows_of_block(b):
        return lambda i: tok[order[b], :, :, columns(i)].reshape(Y * RB, KS // ZL)

    def early(b, k):
        cf[b, k] = partial(rows_of_block(b), (1, 2, 3), k).reshape(Y, RB, HC)

    def product(b, k):
        acc = cf[b, k] + partial(rows_of_block(b), (0,), k).reshape(Y, RB, HC)
        cf[b, k] = acc
        cb[b, k] = acc.astype(jnp.bfloat16)
        send_partial(b, k)

    def product_far(k):
        def a_of(i):
            return jnp.concatenate([tok[xs[2], ys[dy], :, columns(i)] for dy in (1, 2, 3)], axis=0)

        acc = partial(a_of, range(ZL), k)
        for i, dy in enumerate((1, 2, 3)):
            cb[3, k, ys[dy]] = acc[i * RB:(i + 1) * RB].astype(jnp.bfloat16)
        send_partial(3, k)

    def product_last(k):
        cf[3, k, y] = partial(lambda i: tok[xs[2], y, :, columns(i)], range(ZL), k)

    order = (x, xs[3], xs[1], xs[2])

    def total_of(b, k):
        for dy in (1, 3, 2):
            arrived(cin.at[b, k, dy], "c", b, k, dy)
        v = cf[b, k, y]
        for dy in range(1, 4):
            v = v + cin[b, k, dy].astype(jnp.float32)
        dx = (0, 1, 3, 2)[b]
        line = rbuf[dx, :1] if b else rsend[:1]
        line = jnp.broadcast_to(line, (RB, 128))
        return v * jnp.sum(jnp.where(lane == row, line, 0.0), axis=1, keepdims=True)

    def finish(b, k):
        if k == 0:
            if b:
                dx = (0, 1, 3, 2)[b]
                arrived(rbuf.at[dx], "r", dx)
            zs[b] = total_of(b, 0).astype(jnp.bfloat16)
            start(zs.at[b], zin.at[b], partner, "zx", b)
        else:
            out_ref[order[b] * 2 + zh] = (total_of(b, 1) + bias_ref[...]).astype(jnp.bfloat16)

    def own_tokens():
        pltpu.make_async_copy(tok.at[x, y], tok.at[x, y], loc.at[6]).wait()

    def near_tokens():
        arrived(token(3, 3), "xr", 3)
        arrived(token(1, 1), "xl", 1)

    def far_tokens():
        arrived(token(2, 1), "fr", 1)
        arrived(token(2, 3), "fl", 3)
        arrived(token(2, 2, 0), "fr", 2)
        arrived(token(2, 2, 16), "fl", 2)

    def last_tokens():
        arrived(token(2, 0, 0), "fr", 0)
        arrived(token(2, 0, 16), "fl", 0)

    from_y(1)
    from_y(3)
    first_hop_sibling(0)
    first_hop_sibling(1)
    ring(1)
    from_y(2)
    ring(2)
    forward(1)
    ring(3)
    forward(2)
    forward(0)
    ring(4, (0,))
    own_tokens()
    for d in range(1, 4):
        siblings(d)
    ring(4, (1,))
    early(0, 0)
    near_tokens()
    early(1, 0)
    early(2, 0)
    siblings(4, (0,))
    product(0, 0)
    product(1, 0)
    product(2, 0)
    for b in range(3):
        early(b, 1)
    far_tokens()
    product_far(0)
    siblings(4, (1,))
    for b in range(3):
        product(b, 1)
    product_far(1)
    for b in range(3):
        finish(b, 0)
    last_tokens()
    product_last(0)
    finish(3, 0)
    product_last(1)
    for b in range(4):
        finish(b, 1)
    for b in range(4):
        arrived(zin.at[b], "zx", b)
        out_ref[order[b] * 2 + 1 - zh] = (
            zin[b].astype(jnp.float32) + bias_ref[...]
        ).astype(jnp.bfloat16)
    for dst, dev, key in sent:
        copy(dst, dst, dev, *key).wait_send()


def on_device(tokens, gain, stale, bias, first, second, grad, residual, exponent):
    new_first = 0.9 * first + 0.1 * grad
    new_second = 0.95 * second + 0.05 * grad * grad
    vmem = pl.BlockSpec(memory_space=pltpu.VMEM)
    there = pl.BlockSpec(memory_space=pl.ANY)
    bf16, f32 = jnp.bfloat16, jnp.float32
    out = pl.pallas_call(
        kernel,
        out_shape=pltpu.VMEM((8, RB, HC), bf16),
        in_specs=[there, vmem, there, vmem, there, there, there, there, vmem],
        out_specs=vmem,
        scratch_shapes=[
            pltpu.VMEM((RB, 8192), bf16),
            pltpu.VMEM((RB, 2048), f32),
            pltpu.VMEM((RB, 2048), f32),
            pltpu.VMEM((RB, 2048), f32),
            pltpu.VMEM((RB, 2048), f32),
            pltpu.VMEM((X, Y, RB, KS), bf16),
            pltpu.VMEM((ZL, C, X, ZH, 2, RB, HC), bf16),
            pltpu.VMEM((X, RB, HC), bf16),
            pltpu.VMEM((X, RB, HC), bf16),
            pltpu.VMEM((X, 2, RB, HC), bf16),
            pltpu.VMEM((X, 2, RB, HC), bf16),
            pltpu.VMEM((X, 8, 128), f32),
            pltpu.VMEM((8, 128), f32),
            pltpu.VMEM((4, 2, Y, RB, HC), f32),
            pltpu.VMEM((4, 2, Y, RB, HC), bf16),
            pltpu.VMEM((4, 2, Y, RB, HC), bf16),
            pltpu.VMEM((4, RB, HC), bf16),
            pltpu.VMEM((4, RB, HC), bf16),
            pltpu.SemaphoreType.DMA((len(IDS),)),
            pltpu.SemaphoreType.DMA((len(IDS),)),
            pltpu.SemaphoreType.DMA((7,)),
        ],
        compiler_params=pltpu.CompilerParams(collective_id=0, has_side_effects=True),
    )(
        tokens, gain.reshape(64, 128), stale, bias.reshape(1, HC),
        first, second, grad, residual, exponent,
    )
    return (new_first, new_second, out.reshape(256, HC))


def solution(mesh):
    rows = P(("dp", "tensor"), None)
    return jax.shard_map(
        on_device,
        mesh=mesh,
        in_specs=(rows, P(), P(None, "tensor"), P("tensor"), rows, rows, rows, rows, rows),
        out_specs=(rows, rows, P("dp", "tensor")),
        check_vma=False,
    )
```

```python
import jax
import jax.numpy as jnp
from jax import lax
from jax.experimental import pallas as pl
from jax.experimental.pallas import tpu as pltpu
from jax.sharding import PartitionSpec as P

MESH = pl.DeviceIdType.MESH
X, Y, ZL, ZH, C = 4, 4, 4, 2, 2
Z = ZL * ZH
RB = 32
KS = 2048
HC = 256


def ids():
    table = {}

    def add(*key):
        table[key] = len(table)

    add("stale")
    for i in range(1, 4):
        add("r", i)
        add("d", i)
    for p in range(4):
        for half in range(2 if p in (1, 3) else 1):
            if p:
                add("y", p, half)
            add("xr", p, half)
            add("xl", p, half)
    add("fr", 1)
    add("fl", 3)
    for p in (0, 2):
        add("fr", p)
        add("fl", p)
    for h in range(2):
        for d in range(4):
            for cc in range(2):
                add("z", h, d, cc)
        for d in range(5):
            for cc in range(2 if d else 1):
                add("s", h, d, cc)
    for b in range(4):
        add("zx", b)
        for dy in range(1, 4):
            for h in range(2):
                add("c", b, h, dy)
    return table


IDS = ids()


def kernel(
    tok_in, gain_ref, stale_ref, bias_ref, first_in, second_in, grad_in, resid_in, expo_ref,
    out_ref,
    tokv, first_ref, second_ref, grad_ref, resid_ref,
    tok, wbuf, sloc, spart, dsend, drecv, rbuf, rsend, cf, cb, cin, zs, zin, send, recv, loc,
):
    dp = lax.axis_index("dp")
    t = lax.axis_index("tensor")
    c = lax.rem(dp, C)
    y = lax.rem(dp // C, Y)
    zl = dp // (C * Y)
    x = t // ZH
    zh = lax.rem(t, ZH)
    z = zh * ZL + zl

    def at(x_=None, y_=None, z_=None, c_=None):
        x_ = x if x_ is None else x_
        y_ = y if y_ is None else y_
        z_ = z if z_ is None else z_
        c_ = c if c_ is None else c_
        return ((lax.rem(z_, ZL) * Y + y_) * C + c_, x_ * ZH + z_ // ZL)

    xs = [lax.rem(x + i, X) for i in range(X)]
    ys = [lax.rem(y + i, Y) for i in range(Y)]
    zr = [lax.rem(z + i, Z) for i in range(Z)]
    right, left = at(x_=xs[1]), at(x_=xs[3])
    up_z, down_z, sibling = at(z_=zr[1]), at(z_=zr[7]), at(c_=1 - c)
    mirror, partner = at(z_=Z - 1 - z), at(z_=zr[4])

    halves = (1 - zh, zh)

    def copy(src, dst, dev, *key):
        i = IDS[key]
        return pltpu.make_async_remote_copy(
            src_ref=src, dst_ref=dst, send_sem=send.at[i], recv_sem=recv.at[i],
            device_id=dev, device_id_type=MESH,
        )

    sent, sent_last = [], []

    def start(src, dst, dev, *key, late=False):
        copy(src, dst, dev, *key).start()
        if late:
            sent_last.append(key)
        else:
            sent.append((dst, dev, key))

    def arrived(ref, *key):
        copy(ref, ref, right, *key).wait_recv()

    barrier = pltpu.get_barrier_semaphore()
    partners = (
        [mirror, at(x_=xs[2]), at(y_=ys[2]), up_z, down_z, right, left]
        + [at(y_=ys[1]), at(y_=ys[3]), sibling]
    )
    for dev in partners:
        pl.semaphore_signal(barrier, inc=1, device_id=dev, device_id_type=MESH)

    loads = []
    for i, (src, dst) in enumerate((
        (first_in, first_ref), (second_in, second_ref), (grad_in, grad_ref),
        (resid_in, resid_ref), (tok_in, tokv),
    )):
        loads.append(pltpu.make_async_copy(src, dst, loc.at[i]))
        loads[-1].start()

    def stale_rows(dp_, xp, zh_):
        return stale_ref.at[pl.ds(pl.multiple_of(dp_ * 256 + xp * 64 + zh_ * RB, RB), RB), :]

    for xp in range(X):
        pltpu.make_async_copy(stale_rows(dp, xp, zh), sloc.at[xp], loc.at[5]).start()

    for load in loads[:4]:
        load.wait()
    for j in range(16):
        cols = slice(j * 128, (j + 1) * 128)
        g = grad_ref[:, cols]
        nf = 0.9 * first_ref[:, cols] + 0.1 * g
        ns = 0.95 * second_ref[:, cols] + 0.05 * g * g
        corrected = 0.02 * nf / (jnp.sqrt(ns) + 1e-08) + resid_ref[:, cols]
        e = jnp.broadcast_to(expo_ref[:, j:j + 1], (RB, 128))
        up = lax.shift_left(jnp.ones_like(e), e).astype(jnp.float32)
        down = lax.shift_left(jnp.ones_like(e), 30 - e).astype(jnp.float32) * (2.0 ** -30)
        q = jnp.clip(corrected * up, -448.0, 448.0).astype(jnp.bfloat16)
        dsend[j // 4, (j // 2) % 2, :, (j % 2) * 128:(j % 2 + 1) * 128] = (
            q.astype(jnp.float32) * down
        ).astype(jnp.bfloat16)

    lane = lax.broadcasted_iota(jnp.int32, (RB, 128), 1)
    row = lax.broadcasted_iota(jnp.int32, (RB, 128), 0)
    gcol = []
    for xp in range(X):
        grow = jnp.broadcast_to(gain_ref[pl.ds(dp * 2 + xp // 2, 1), :], (RB, 128))
        hit = lane == row + (xp % 2) * 64 + zh * RB
        gcol.append(jnp.sum(jnp.where(hit, grow, 0.0), axis=1, keepdims=True))

    loads[4].wait()
    total = jnp.zeros((RB, 1), jnp.float32)
    for k in range(8):
        v = tokv[:, k * 1024:(k + 1) * 1024].astype(jnp.float32)
        total = total + jnp.sum(v * v, axis=1, keepdims=True)
    scale = lax.rsqrt(total / 8192.0 + 1e-06)
    rsend[...] = jnp.broadcast_to(
        jnp.sum(jnp.where(lane == row, scale, 0.0), axis=0, keepdims=True), (8, 128)
    )

    pl.semaphore_wait(barrier, len(partners))

    for dx in (1, 3, 2):
        start(dsend.at[xs[dx]], drecv.at[dx], at(x_=xs[dx]), "d", dx)
    dp_m = ((ZL - 1 - zl) * Y + y) * C + c
    for xp in range(X):
        copy(stale_rows(dp_m, xp, 1 - zh), spart.at[xp], mirror, "stale").start()
    sent.append((spart, mirror, ("stale",)))

    def part(k, y_, rows=slice(None)):
        return tokv.at[rows, pl.ds(pl.multiple_of(k * 2048 + y_ * 512, 512), 512)]

    def rows_of(p, half):
        return pl.ds(half * 16, 16) if p in (1, 3) else slice(None)

    def spread(dev, y_, *key):
        rows = rows_of(*key[1:])
        for k in range(ZL):
            dst = tok.at[x, y, rows, pl.ds(k * 512, 512)]
            copy(part(k, y_, rows), dst, dev, *key).start()
        sent.append((tok.at[x, y, rows], dev, key))

    spread(at(y_=ys[1]), ys[1], "y", 1, 0)
    spread(at(y_=ys[3]), ys[3], "y", 3, 0)
    spread(right, y, "xr", 0, 0)
    spread(left, y, "xl", 0, 0)
    spread(at(y_=ys[1]), ys[1], "y", 1, 1)
    spread(at(y_=ys[3]), ys[3], "y", 3, 1)
    spread(at(y_=ys[2]), ys[2], "y", 2, 0)
    for k in range(ZL):
        pltpu.make_async_copy(part(k, y), tok.at[x, y, :, pl.ds(k * 512, 512)], loc.at[6]).start()
    for dx in range(1, 4):
        start(rsend, rbuf.at[dx], at(x_=xs[dx]), "r", dx)

    def merge(dx, half, stale):
        xp = xs[(4 - dx) % 4]
        d = dsend[xp, half] if dx == 0 else drecv[dx, half]
        g = gcol[3]
        for i in range(3):
            g = jnp.where(xp == i, gcol[i], g)
        w = g * (stale[xp].astype(jnp.float32) + d.astype(jnp.float32))
        wbuf[zl, c, xp, zh, half] = w.astype(jnp.bfloat16)

    way = 1 - 2 * c
    onward = at(z_=lax.rem(z + way + Z, Z))

    def block(hops, core, h):
        z_ = lax.rem(z + way * hops + 2 * Z, Z)
        zh_ = z_ // ZL
        return wbuf.at[lax.rem(z_, ZL), core, :, zh_, 1 - zh_ if h else zh_]

    def first_hop(h):
        ref = block(0, c, h)
        start(ref, ref, sibling, "s", h, 0, 0)
        start(ref, ref, onward, "z", h, 0, 0)

    def first_hop_sibling(h):
        ref = block(0, 1 - c, h)
        arrived(ref, "s", h, 0, 0)
        start(ref, ref, onward, "z", h, 0, 1)

    pltpu.make_async_copy(sloc, sloc, loc.at[5]).wait()
    merge(0, zh, sloc)
    for dx in (1, 3, 2):
        arrived(drecv.at[dx], "d", dx)
        merge(dx, zh, sloc)
    def from_y(p, half=0):
        ref = tok.at[x, ys[(4 - p) % 4], rows_of(p, half)]
        arrived(ref, "y", p, half)
        start(ref, ref, right, "xr", p, half)
        start(ref, ref, left, "xl", p, half)

    def token(i, p, rows=None):
        ref = tok.at[xs[i], ys[(4 - p) % 4]]
        return ref if rows is None else ref.at[pl.ds(rows, RB // 2), :]

    def landed(i, p, name):
        for half in range(2 if p in (1, 3) else 1):
            arrived(tok.at[xs[i], ys[(4 - p) % 4], rows_of(p, half)], name, p, half)

    first_hop(0)
    from_y(1, 0)
    from_y(3, 0)
    arrived(spart, "stale")
    for dx in (0, 1, 3, 2):
        merge(dx, 1 - zh, spart)
    first_hop(1)

    def ring(d):
        for cc in range(2):
            for h in range(2):
                ref = block(-d, 1 - c if cc else c, h)
                arrived(ref, "z", h, d - 1, cc)
                if d < 3:
                    start(ref, ref, onward, "z", h, d, cc)
                elif d == 3:
                    last_hop(ref, h, cc)
                start(ref, ref, sibling, "s", h, d, cc, late=d == 4)

    def last_hop(ref, h, cc):
        @pl.when(c == 1)
        def _():
            start(ref, ref, onward, "z", h, 3, cc, late=True)

    def forward(p):
        if p == 1:
            landed(3, 1, "xr")
            start(token(3, 1), token(3, 1), right, "fr", 1)
            landed(1, 3, "xl")
            start(token(1, 3), token(1, 3), left, "fl", 3)
        else:
            landed(3, p, "xr")
            start(token(3, p, 0), token(3, p, 0), right, "fr", p)
            landed(1, p, "xl")
            start(token(1, p, 16), token(1, p, 16), left, "fl", p)

    def siblings(d, hs=(0, 1)):
        for cc in range(2):
            for h in hs:
                arrived(block(d, c if cc else 1 - c, h), "s", h, d, cc)

    def last_ring():
        @pl.when(c == 1)
        def _():
            ring(4)

    def last_siblings(h):
        @pl.when(c == 0)
        def _():
            siblings(4, (h,))

    def quarter(i, k):
        return wbuf[zls[i], :, :, :, halves[k]].reshape(KS // ZL, HC)

    zls = [lax.rem(zl + i, ZL) for i in range(ZL)]

    def columns(i):
        return pl.ds(pl.multiple_of(zls[i] * 512, 512), 512)

    def partial(a_of, ks, k):
        acc = None
        for i in ks:
            one = jnp.dot(a_of(i), quarter(i, k), preferred_element_type=jnp.float32)
            acc = one if acc is None else acc + one
        return acc

    def send_partial(b, h):
        for dy in (1, 3, 2):
            start(cb.at[b, h, ys[dy]], cin.at[b, h, dy], at(y_=ys[dy]), "c", b, h, dy)

    def rows_of_block(b):
        return lambda i: tok[order[b], :, :, columns(i)].reshape(Y * RB, KS // ZL)

    def early(b, k):
        cf[b, k] = partial(rows_of_block(b), (1, 2, 3), k).reshape(Y, RB, HC)

    def product(b, k):
        acc = cf[b, k] + partial(rows_of_block(b), (0,), k).reshape(Y, RB, HC)
        cf[b, k] = acc
        cb[b, k] = acc.astype(jnp.bfloat16)
        send_partial(b, k)

    def product_far(k):
        def a_of(i):
            return jnp.concatenate([tok[xs[2], ys[dy], :, columns(i)] for dy in (1, 2, 3)], axis=0)

        acc = partial(a_of, range(ZL), k)
        for i, dy in enumerate((1, 2, 3)):
            cb[3, k, ys[dy]] = acc[i * RB:(i + 1) * RB].astype(jnp.bfloat16)
        send_partial(3, k)

    def product_last(k):
        cf[3, k, y] = partial(lambda i: tok[xs[2], y, :, columns(i)], range(ZL), k)

    order = (x, xs[3], xs[1], xs[2])

    def total_of(b, k):
        for dy in (1, 3, 2):
            arrived(cin.at[b, k, dy], "c", b, k, dy)
        v = cf[b, k, y]
        for dy in range(1, 4):
            v = v + cin[b, k, dy].astype(jnp.float32)
        dx = (0, 1, 3, 2)[b]
        line = rbuf[dx, :1] if b else rsend[:1]
        line = jnp.broadcast_to(line, (RB, 128))
        return v * jnp.sum(jnp.where(lane == row, line, 0.0), axis=1, keepdims=True)

    def finish(b, k):
        if k == 0:
            if b:
                dx = (0, 1, 3, 2)[b]
                arrived(rbuf.at[dx], "r", dx)
            zs[b] = total_of(b, 0).astype(jnp.bfloat16)
            start(zs.at[b], zin.at[b], partner, "zx", b)
        else:
            out_ref[order[b] * 2 + zh] = (total_of(b, 1) + bias_ref[...]).astype(jnp.bfloat16)

    def own_tokens():
        pltpu.make_async_copy(tok.at[x, y], tok.at[x, y], loc.at[6]).wait()

    def near_tokens():
        landed(3, 3, "xr")
        landed(1, 1, "xl")

    def far_tokens():
        arrived(token(2, 1), "fr", 1)
        arrived(token(2, 3), "fl", 3)
        arrived(token(2, 2, 0), "fr", 2)
        arrived(token(2, 2, 16), "fl", 2)

    def last_tokens():
        arrived(token(2, 0, 0), "fr", 0)
        arrived(token(2, 0, 16), "fl", 0)

    from_y(1, 1)
    from_y(3, 1)
    first_hop_sibling(0)
    first_hop_sibling(1)
    ring(1)
    from_y(2)
    ring(2)
    forward(1)
    ring(3)
    forward(2)
    forward(0)
    last_ring()
    own_tokens()
    for d in range(1, 4):
        siblings(d)
    early(0, 0)
    near_tokens()
    early(1, 0)
    early(2, 0)
    last_siblings(0)
    product(0, 0)
    product(1, 0)
    product(2, 0)
    for b in range(3):
        early(b, 1)
    far_tokens()
    product_far(0)
    last_siblings(1)
    for b in range(3):
        product(b, 1)
    product_far(1)
    for b in range(3):
        finish(b, 0)
    last_tokens()
    product_last(0)
    finish(3, 0)
    product_last(1)
    for b in range(4):
        finish(b, 1)
    for b in range(4):
        arrived(zin.at[b], "zx", b)
        out_ref[order[b] * 2 + 1 - zh] = (
            zin[b].astype(jnp.float32) + bias_ref[...]
        ).astype(jnp.bfloat16)
    for dst, dev, key in sent:
        copy(dst, dst, dev, *key).wait_send()

    @pl.when(c == 1)
    def _():
        for key in sent_last:
            copy(block(4, c, 0), block(4, c, 0), sibling, *key).wait_send()


def on_device(tokens, gain, stale, bias, first, second, grad, residual, exponent):
    new_first = 0.9 * first + 0.1 * grad
    new_second = 0.95 * second + 0.05 * grad * grad
    vmem = pl.BlockSpec(memory_space=pltpu.VMEM)
    there = pl.BlockSpec(memory_space=pl.ANY)
    bf16, f32 = jnp.bfloat16, jnp.float32
    out = pl.pallas_call(
        kernel,
        out_shape=pltpu.VMEM((8, RB, HC), bf16),
        in_specs=[there, vmem, there, vmem, there, there, there, there, vmem],
        out_specs=vmem,
        scratch_shapes=[
            pltpu.VMEM((RB, 8192), bf16),
            pltpu.VMEM((RB, 2048), f32),
            pltpu.VMEM((RB, 2048), f32),
            pltpu.VMEM((RB, 2048), f32),
            pltpu.VMEM((RB, 2048), f32),
            pltpu.VMEM((X, Y, RB, KS), bf16),
            pltpu.VMEM((ZL, C, X, ZH, 2, RB, HC), bf16),
            pltpu.VMEM((X, RB, HC), bf16),
            pltpu.VMEM((X, RB, HC), bf16),
            pltpu.VMEM((X, 2, RB, HC), bf16),
            pltpu.VMEM((X, 2, RB, HC), bf16),
            pltpu.VMEM((X, 8, 128), f32),
            pltpu.VMEM((8, 128), f32),
            pltpu.VMEM((4, 2, Y, RB, HC), f32),
            pltpu.VMEM((4, 2, Y, RB, HC), bf16),
            pltpu.VMEM((4, 2, Y, RB, HC), bf16),
            pltpu.VMEM((4, RB, HC), bf16),
            pltpu.VMEM((4, RB, HC), bf16),
            pltpu.SemaphoreType.DMA((len(IDS),)),
            pltpu.SemaphoreType.DMA((len(IDS),)),
            pltpu.SemaphoreType.DMA((7,)),
        ],
        compiler_params=pltpu.CompilerParams(collective_id=0, has_side_effects=True),
    )(
        tokens, gain.reshape(64, 128), stale, bias.reshape(1, HC),
        first, second, grad, residual, exponent,
    )
    return (new_first, new_second, out.reshape(256, HC))


def solution(mesh):
    rows = P(("dp", "tensor"), None)
    return jax.shard_map(
        on_device,
        mesh=mesh,
        in_specs=(rows, P(), P(None, "tensor"), P("tensor"), rows, rows, rows, rows, rows),
        out_specs=(rows, rows, P("dp", "tensor")),
        check_vma=False,
    )
```
